256 devices in a mesh: batch: 8 (over z), col: 32 (over y, x, core).
Axes of the slice: x: 4, y: 4, z: 8, core: 2. Of those that a mesh axis runs over, the one named last changes fastest.
Arguments:
- views: bfloat16 [2, 1024, 4096], P(None, 'batch', 'col'), may hold values from -132 to 132
- norm_scale_gain: float32 [4096], P('col'), may hold values from 0.5 to 1.5
- norm_shift_bias: float32 [4096], P('col'), may hold values from -3 to 3
- weight: bfloat16 [4096, 8192], P(None, 'col'), may hold values from -0.09375 to 0.09375
Outputs:
- loss: float32 [], replicated
- grad_weight: float32 [4096, 8192], P('batch', 'col')
- grad_gain: float32 [4096], P('col')
- grad_bias: float32 [4096], P('col')
- views_gradient: float32 [2, 1024, 4096], P(None, 'batch', 'col')
The draws below stay inside these ranges and needn't reach their ends.
All inputs are finite; a program needn't handle non-finite values.
Results may differ from the reference program's by a relative error of at most 0.0027.
Values may be sent and summed in bfloat16 or wider, within the bound.
A program may use at most 64 MiB of HBM per device.

```python
import jax
import jax.numpy as jnp
from jax import lax

H = 4096
E = 8192
PAIRS = 1024


def draw_views(key, part):
    keys = jax.random.split(key, 6)
    rank = jnp.arange(PAIRS, dtype=jnp.float32) / float(PAIRS - 1)
    row_noise = jax.random.uniform(keys[0], (2, PAIRS, 1), dtype=jnp.float32)
    row_scale = jnp.exp(jnp.log(3.0) * rank[None, :, None] + jnp.log(3.5) * row_noise)
    col_scale = 0.3 * jnp.exp(jnp.log(10.0) * jax.random.uniform(keys[1], (1, 1, H), dtype=jnp.float32))
    noise = jax.random.truncated_normal(keys[2], -4.0, 4.0, (2, PAIRS, H), dtype=jnp.float32)
    centre = jax.random.uniform(keys[5], (1, 1, H), dtype=jnp.float32, minval=-2.0, maxval=2.0)
    return (col_scale * (row_scale * noise + centre)).astype(jnp.bfloat16)


def shard_levels(own_key, dims, cuts, smallest, largest):
    gain = 1.0
    for position, parts in cuts:
        steps = jax.random.uniform(jax.random.fold_in(jax.random.fold_in(own_key, 6), position), (parts,), jnp.float32, smallest / len(cuts), largest / len(cuts))
        gain = gain * jnp.repeat(jnp.exp(steps), dims[position] // parts).reshape((-1,) + (1,) * (len(dims) - 1 - position))
    return gain


def bell_draw(own_key, dims, scale, most, cuts=(), kind=jnp.bfloat16):
    values = jax.random.normal(own_key, dims, jnp.float32) * scale
    if len(cuts) > 0:
        values = shard_levels(own_key, dims, cuts, -0.22, 0.18) * values
    return jnp.clip(values, min=-most, max=most).astype(kind)


def setup_inputs(seed: int = 0) -> dict:
    splits = jax.random.split(jax.random.key(seed), 5)
    views = draw_views(jax.random.fold_in(splits[4], 71), 0)
    norm_scale_gain = jnp.clip(1.0 + 0.1 * jax.random.normal(splits[1], (H,), jnp.float32), 0.5, 1.5)
    norm_shift_bias = bell_draw(splits[2], (H,), 0.5, 3.0, ((0, 32),), jnp.float32)
    weight = bell_draw(splits[3], (H, E), H ** -0.5, 0.09375, ((1, 32),))
    return dict(views=views, norm_scale_gain=norm_scale_gain, norm_shift_bias=norm_shift_bias, weight=weight)


eps_norm = 1e-05
eps_std = 0.0001

def gelu_slope(preactivation):
    value, pullback = jax.vjp(lambda t: jax.nn.gelu(t, approximate=True), preactivation)
    return pullback(jnp.ones_like(value))[0]

def reference(views, norm_scale_gain, norm_shift_bias, weight):
    sample_count = PAIRS
    scale = PAIRS * E / 128.0
    hidden_float = views.astype(jnp.float32)
    batch_average = lax.optimization_barrier(jnp.mean(hidden_float, axis=1, keepdims=True))
    var = lax.optimization_barrier(jnp.mean((hidden_float - batch_average) * (hidden_float - batch_average), axis=1, keepdims=True))
    inverse_deviation = 1.0 / jnp.sqrt(var + eps_norm)
    normalised_input = (hidden_float - batch_average) * inverse_deviation
    preactivation = norm_scale_gain * normalised_input + norm_shift_bias
    act = jax.nn.gelu(preactivation, approximate=True).astype(jnp.bfloat16)
    z = jnp.stack([jnp.dot(act[v], weight, preferred_element_type=jnp.float32) for v in range(2)]).astype(jnp.bfloat16)
    zf = z.astype(jnp.float32)
    zmean = lax.optimization_barrier(jnp.mean(zf, axis=1, keepdims=True))
    zc = zf - zmean
    zvar = lax.optimization_barrier(jnp.sum(zc * zc, axis=1, keepdims=True)) / (sample_count - 1)
    std = jnp.sqrt(zvar + eps_std)
    zcb = zc.astype(jnp.bfloat16)
    diff = zf[0] - zf[1]
    invariance = jnp.sum(diff * diff) / (sample_count * E)
    hinge = jnp.sum(jnp.maximum(1.0 - std, 0.0)) / (2 * E)
    denom = float((sample_count - 1) ** 2 * E)
    coef = 4.0 * scale / denom
    hinge_coef = 25.0 * scale / (2.0 * E * (sample_count - 1))
    loss_cov = jnp.float32(0.0)
    grads = []
    for v in range(2):
        kernel = jnp.dot(zcb[v], zcb[v].T, preferred_element_type=jnp.float32)
        diag = lax.optimization_barrier(jnp.sum(jnp.square(zcb[v].astype(jnp.float32)), axis=0, keepdims=True))
        loss_cov = loss_cov + (jnp.sum(kernel * kernel) - jnp.sum(diag * diag)) / denom
        moved = jnp.dot(kernel.astype(jnp.bfloat16), zcb[v], preferred_element_type=jnp.float32)
        g_cov = coef * (moved - zcb[v].astype(jnp.float32) * diag)
        mask = jnp.where(std[v] < 1.0, 1.0, 0.0)
        g_var = -hinge_coef * mask * zc[v] / std[v]
        summed = g_cov + g_var
        grads.append(summed - lax.optimization_barrier(jnp.mean(summed, axis=0, keepdims=True)))
    g_inv = 50.0 * scale / (sample_count * E) * diff
    dz = (jnp.stack(grads) + jnp.stack([g_inv, -g_inv])).astype(jnp.bfloat16)
    loss = 25.0 * invariance + 25.0 * hinge + loss_cov
    act_flat = act.reshape(2 * sample_count, H)
    dz_flat = dz.reshape(2 * sample_count, E)
    grad_weight = jnp.dot(act_flat.T, dz_flat, preferred_element_type=jnp.float32)
    d_act = jnp.dot(dz_flat, weight.T, preferred_element_type=jnp.float32).reshape(2, sample_count, H)
    preactivation_gradient = d_act * gelu_slope(preactivation)
    bias_gradient_sum = lax.optimization_barrier(jnp.sum(preactivation_gradient, axis=1, keepdims=True))
    gain_gradient_sum = lax.optimization_barrier(jnp.sum(preactivation_gradient * normalised_input, axis=1, keepdims=True))
    grad_bias = lax.optimization_barrier(jnp.sum(bias_gradient_sum, axis=(0, 1)))
    grad_gain = lax.optimization_barrier(jnp.sum(gain_gradient_sum, axis=(0, 1)))
    views_gradient = norm_scale_gain * (preactivation_gradient - bias_gradient_sum / sample_count - normalised_input * gain_gradient_sum / sample_count) * inverse_deviation
    return (loss, grad_weight, grad_gain, grad_bias, views_gradient)
```

```python
import jax
import jax.numpy as jnp
from jax import lax
from jax.experimental import pallas as pl
from jax.experimental.pallas import tpu as pltpu
from jax.sharding import PartitionSpec as P

E = 8192
ROWS = 1024
PLANES = 8
SIDE = 4

eps_norm = 1e-05
eps_std = 0.0001
scale = ROWS * E / 128.0
denom = float((ROWS - 1) ** 2 * E)
coef = 4.0 * scale / denom
hinge_coef = 25.0 * scale / (2.0 * E * (ROWS - 1))
inv_coef = 50.0 * scale / (ROWS * E)

F32 = jnp.float32
BF16 = jnp.bfloat16
MESH = pl.DeviceIdType.MESH


def dot_nt(a, b):
    return lax.dot_general(a, b, (((1,), (1,)), ((), ())), preferred_element_type=F32)


def dot_tn(a, b):
    return lax.dot_general(a, b, (((0,), (0,)), ((), ())), preferred_element_type=F32)


def dot_nn(a, b):
    return jnp.dot(a, b, preferred_element_type=F32)


class Net:
    def __init__(self, send, recv):
        self.send, self.recv, self.sent = send, recv, []
        self.z = lax.axis_index("batch")
        self.c = lax.axis_index("col")
        self.core = lax.rem(self.c, 2)
        self.chip = lax.div(self.c, 2)
        self.x = lax.rem(self.chip, SIDE)
        self.y = lax.div(self.chip, SIDE)

    def at_z(self, d):
        return (lax.rem(self.z + d, PLANES), self.c)

    def at(self, y, x):
        return (self.z, (y * SIDE + x) * 2 + self.core)

    def along(self, h, f, t):
        return self.at(t, f) if h == 0 else self.at(f, t)

    def partner(self):
        return (self.z, self.chip * 2 + 1 - self.core)

    def push(self, src, dst, device):
        i = len(self.sent)
        copy = pltpu.make_async_remote_copy(
            src_ref=src,
            dst_ref=dst,
            send_sem=self.send.at[i],
            recv_sem=self.recv.at[i],
            device_id=device,
            device_id_type=MESH,
        )
        copy.start()
        self.sent.append(copy)
        return copy

    def peers(self):
        found = [self.partner()]
        found += [self.at_z(d) for d in range(1, PLANES)]
        found += [self.at(self.y, lax.rem(self.x + d, SIDE)) for d in range(1, SIDE)]
        found += [self.at(lax.rem(self.y + d, SIDE), self.x) for d in range(1, SIDE)]
        return found


def mod4(a):
    return lax.rem(a, SIDE)


def mod8(a):
    return lax.rem(a, PLANES)


def share_z(net, buf):
    sent = [net.push(buf.at[net.z], buf.at[net.z], net.at_z(d)) for d in range(1, PLANES)]
    yield
    for copy in sent:
        copy.wait_recv()
    yield


def ring_z(net, buf):
    up, down = {}, {}
    for v in range(2):
        up[1, v] = net.push(buf.at[net.z, v], buf.at[net.z, v], net.at_z(1))
        down[1, v] = net.push(buf.at[net.z, v], buf.at[net.z, v], net.at_z(7))
    yield
    for d in range(1, 5):
        for v in range(2):
            if d < 4 or v == 0:
                up[d, v].wait_recv()
                if d < 3 or (d == 3 and v == 0):
                    block = buf.at[mod8(net.z + 8 - d), v]
                    up[d + 1, v] = net.push(block, block, net.at_z(1))
            if d < 4 or v == 1:
                down[d, v].wait_recv()
                if d < 3 or (d == 3 and v == 1):
                    block = buf.at[mod8(net.z + d), v]
                    down[d + 1, v] = net.push(block, block, net.at_z(7))
        yield


def gather_plane(net, buf, forward):
    first_at, then_at = (net.x, net.y), (net.y, net.x)

    def piece(h, f, t, s=None):
        y, x = (t, f) if h == 0 else (f, t)
        return buf.at[y, x, net.core, h] if s is None else buf.at[y, x, net.core, h, s]

    def line(h, f):
        return buf.at[:, f, net.core, 0] if h == 0 else buf.at[f, :, net.core, 1]

    def send(h, f, t, s, df, dt):
        block = piece(h, f, t, s)
        return net.push(block, block, net.along(h, mod4(first_at[h] + df), mod4(then_at[h] + dt)))

    reach = (1, 3) if forward else (1, 3, 2)
    shift = (0, 3, 1, 2)
    first, cross, tie1, tie2, over = {}, {}, {}, {}, []

    def spread(h, j):
        f = mod4(first_at[h] + shift[j])
        for d in reach:
            cross[h, j, d] = send(h, f, then_at[h], None, 0, d)

    def finish(h, j):
        f = mod4(first_at[h] + shift[j])
        for d in reach:
            cross[h, j, d].wait_recv()
            if forward:
                s = 0 if d == 1 else 1
                tie2[h, j, s] = send(h, f, mod4(then_at[h] + 4 - d), s, 0, d)

    def hand_over(h, j):
        if forward:
            for s in range(2):
                tie2[h, j, s].wait_recv()
        f = mod4(first_at[h] + shift[j])
        over.append(net.push(line(h, f), line(h, f), net.partner()))

    for h in range(2):
        for d in reach:
            first[h, d] = send(h, first_at[h], then_at[h], None, d, 0)
    for h in range(2):
        spread(h, 0)
    yield
    for h in range(2):
        first[h, 1].wait_recv()
        if forward:
            tie1[h, 0] = send(h, mod4(first_at[h] + 3), then_at[h], 0, 1, 0)
        spread(h, 1)
        first[h, 3].wait_recv()
        if forward:
            tie1[h, 1] = send(h, mod4(first_at[h] + 1), then_at[h], 1, 3, 0)
        spread(h, 2)
    for h in range(2):
        finish(h, 0)
    yield
    for h in range(2):
        if forward:
            tie1[h, 0].wait_recv()
            tie1[h, 1].wait_recv()
        else:
            first[h, 2].wait_recv()
        spread(h, 3)
    for h in range(2):
        finish(h, 1)
        finish(h, 2)
        hand_over(h, 0)
    yield
    for h in range(2):
        finish(h, 3)
        hand_over(h, 1)
        hand_over(h, 2)
    for h in range(2):
        hand_over(h, 3)
    yield
    for copy in over:
        copy.wait_recv()
    yield


def reduce_plane(net, part_ref, tie1, full1, mid, tie2, full2, out):
    first_at, then_at = (net.x, net.y), (net.y, net.x)

    def part(h, f, lo, n=2):
        return part_ref.at[0, :, lo : lo + n, f] if h == 0 else part_ref.at[1, :, f, lo : lo + n]

    def first_dev(h, d):
        return net.along(h, mod4(first_at[h] + d), then_at[h])

    def then_dev(h, d):
        return net.along(h, first_at[h], mod4(then_at[h] + d))

    a, b = {}, {}
    for h in range(2):
        f = first_at[h]
        a[h, 0] = net.push(part(h, mod4(f + 2), 0), tie1.at[h, 0], first_dev(h, 1))
        a[h, 1] = net.push(part(h, mod4(f + 2), 2), tie1.at[h, 1], first_dev(h, 3))
    for h in range(2):
        f = first_at[h]
        a[h, 2] = net.push(part(h, mod4(f + 1), 2), full1.at[h, 0, :, 2:4], first_dev(h, 1))
        a[h, 3] = net.push(part(h, mod4(f + 3), 0), full1.at[h, 1, :, 0:2], first_dev(h, 3))
    yield
    for h in range(2):
        f = first_at[h]
        for k, lo in ((0, 0), (1, 2)):
            d = 1 if k == 0 else 3
            a[h, k].wait_recv()
            mine = part(h, mod4(f + d), lo)
            mine[...] = (mine[...].astype(F32) + tie1[h, k].astype(F32)).astype(mine.dtype)
            a[h, 4 + k] = net.push(mine, full1.at[h, k, :, lo : lo + 2], first_dev(h, d))
    yield
    for h in range(2):
        f, t = first_at[h], then_at[h]
        for k in range(2, 6):
            a[h, k].wait_recv()
        mine = part(h, f, 0, 4)
        mid[h] = mine[...].astype(F32) + full1[h, 0].astype(F32) + full1[h, 1].astype(F32)
        b[h, 0] = net.push(mid.at[h, 0, mod4(t + 2)], tie2.at[h, 0], then_dev(h, 1))
        b[h, 1] = net.push(mid.at[h, 1, mod4(t + 2)], tie2.at[h, 1], then_dev(h, 3))
        b[h, 2] = net.push(mid.at[h, 1, mod4(t + 1)], full2.at[h, 0, 1], then_dev(h, 1))
        b[h, 3] = net.push(mid.at[h, 0, mod4(t + 3)], full2.at[h, 1, 0], then_dev(h, 3))
    yield
    for h in range(2):
        t = then_at[h]
        for k in range(2):
            d = 1 if k == 0 else 3
            b[h, k].wait_recv()
            mine = mid.at[h, k, mod4(t + d)]
            mine[...] = mine[...] + tie2[h, k]
            b[h, 4 + k] = net.push(mine, full2.at[h, k, k], then_dev(h, d))
    yield
    for h in range(2):
        for k in range(2, 6):
            b[h, k].wait_recv()
        out[h] = mid[h, :, then_at[h]] + full2[h, 0] + full2[h, 1]
    yield


def rows_of(parts, width):
    count = len(parts)
    rows = list(parts)
    if count < 8:
        rows.append(jnp.zeros((8 - count, width), F32))
    return jnp.concatenate(rows, axis=0)


def col_sum(t):
    return jnp.sum(t, axis=0, keepdims=True)


def body(
    views,
    gain,
    bias,
    w_hbm,
    loss,
    grad_weight,
    grad_gain,
    grad_bias,
    views_gradient,
    w,
    act,
    act_t,
    xhat,
    slope,
    stats,
    zacc,
    zbuf,
    zsum,
    zcb,
    colstat,
    kpart,
    krecv,
    ktie1,
    kfull1,
    kmid,
    ktie2,
    kfull2,
    kown,
    kgat,
    summed,
    gsum,
    dz,
    dgive,
    dkeep,
    drecv,
    dpart,
    dtie1,
    dfull1,
    dmid,
    dtie2,
    dfull2,
    dact,
    lsend,
    lrecv,
    fstat,
    send_sems,
    recv_sems,
    load_sem,
):
    net = Net(send_sems, recv_sems)
    z, y, x, core, chip = net.z, net.y, net.x, net.core, net.chip
    load = pltpu.make_async_copy(w_hbm, w, load_sem)
    load.start()
    barrier = pltpu.get_barrier_semaphore()
    peers = net.peers()
    for peer in peers:
        pl.semaphore_signal(barrier, inc=1, device_id=peer, device_id_type=MESH)
    local = []
    for v in range(2):
        t = views[v].astype(F32)
        m = col_sum(t) / 128.0
        local.append((m, col_sum((t - m) * (t - m))))
    stats[z] = rows_of([local[0][0], local[1][0], local[0][1], local[1][1]], 128)
    pl.semaphore_wait(barrier, len(peers))

    g = share_z(net, stats)
    next(g)
    next(g)
    inverse = []
    for v in range(2):
        m = stats[:, v, :]
        mean = col_sum(m) / PLANES
        spread = col_sum(stats[:, 2 + v, :] + 128.0 * (m - mean) * (m - mean))
        inv = 1.0 / jnp.sqrt(spread / ROWS + eps_norm)
        inverse.append(inv)
        xh = (views[v].astype(F32) - mean) * inv
        pre = gain[...] * xh + bias[...]
        inner = 0.7978845608028654 * (pre + 0.044715 * (pre * pre * pre))
        th = jnp.tanh(inner)
        a = 0.5 * pre * (1.0 + th)
        act[y, x, core, v] = a.astype(BF16).reshape(2, 4, 16, 128)
        xhat[v] = xh
        slope[v] = 0.5 * (1.0 + th) + 0.5 * pre * (1.0 - th * th) * (
            0.7978845608028654 * (1.0 + 3.0 * 0.044715 * (pre * pre))
        )

    for _ in gather_plane(net, act, True):
        pass

    row_v, row_s, row_q = lax.div(chip, 8), lax.rem(lax.div(chip, 4), 2), lax.rem(chip, 4)

    def feature_rows(plane):
        owner = plane * 2 + core
        return act.at[lax.div(owner, 4), lax.rem(owner, 4), :, row_v, row_s, row_q]

    own_rows = act_t.at[y, x, core, :, lax.div(z, 4), lax.rem(z, 4)]
    moved_rows = []
    for d in range(1, PLANES):
        moved_rows.append(net.push(feature_rows(mod8(z + d)), own_rows, net.at_z(d)))
    own_rows[...] = feature_rows(z)[...]

    load.wait()
    zacc[...] = jnp.zeros_like(zacc)

    def z_step(i, carry):
        cy, cx = lax.div(i, 4), lax.rem(i, 4)
        lhs = jnp.concatenate(
            [act[cy, cx, 0].reshape(256, 128), act[cy, cx, 1].reshape(256, 128)], axis=1
        )
        zacc[...] += dot_nn(lhs, w[pl.ds(pl.multiple_of(i * 256, 256), 256), :])
        return carry

    lax.fori_loop(0, 16, z_step, 0)
    zb = zacc[...].astype(BF16)
    zbuf[z] = zb.reshape(2, 128, 256)
    zf = zb.astype(F32)
    zsum[z] = rows_of([col_sum(zf[0:128]), col_sum(zf[128:256])], 256)

    means = share_z(net, zsum)
    next(means)
    zring = ring_z(net, zbuf)
    next(zring)
    for copy in moved_rows:
        copy.wait_recv()
    agt = gather_plane(net, act_t, True)
    next(agt)
    next(means)
    zmean = [col_sum(zsum[:, v, :]) / ROWS for v in range(2)]
    colstat[...] = jnp.zeros_like(colstat)

    def block_in(slot):
        for v in range(2):
            zc = zbuf[slot, v].astype(F32) - zmean[v]
            cb = zc.astype(BF16)
            zcb[slot, v] = cb
            cf = cb.astype(F32)
            colstat[v : v + 1, :] += col_sum(zc * zc)
            colstat[2 + v : 3 + v, :] += col_sum(cf * cf)
            kb = dot_nt(zcb[z, v], cb)
            kpart[lax.div(slot, 4), lax.rem(lax.div(slot, 2), 2), lax.rem(slot, 2), 2 * v : 2 * v + 2] = kb.reshape(
                2, 4, 16, 128
            )

    block_in(z)
    next(agt)
    next(zring)
    block_in(mod8(z + 7))
    block_in(mod8(z + 1))
    next(agt)
    next(zring)
    block_in(mod8(z + 6))
    block_in(mod8(z + 2))
    next(agt)
    next(zring)
    block_in(mod8(z + 5))
    block_in(mod8(z + 3))
    next(zring)
    block_in(mod8(z + 4))

    over = net.push(kpart.at[1 - core], krecv, net.partner())
    over.wait_recv()
    mine = kpart.at[core]
    mine[...] = mine[...] + krecv[...]
    for _ in reduce_plane(net, mine, ktie1, kfull1, kmid, ktie2, kfull2, kown):
        pass
    kgat[y, x, core] = kown[...].astype(BF16)
    gk = gather_plane(net, kgat, False)
    next(gk)
    next(agt)
    ksq = kown[...] * kown[...]
    ksq = col_sum(jnp.sum(ksq, axis=(0, 1)))
    for _ in gk:
        pass

    hinge_row = jnp.zeros((1, 256), F32)
    diag_row = jnp.zeros((1, 256), F32)
    local_sum = []
    for v in range(2):
        std = jnp.sqrt(colstat[v : v + 1, :] / (ROWS - 1) + eps_std)
        diag = colstat[2 + v : 3 + v, :]
        hinge_row = hinge_row + jnp.maximum(1.0 - std, 0.0)
        diag_row = diag_row + diag * diag
        moved = jnp.zeros((128, 256), F32)
        for b in range(0, 8, 2):
            lhs = jnp.concatenate(
                [
                    kgat[2 * v : 2 * v + 2, :, q // 4, (q // 2) % 2, q % 2].reshape(128, 128)
                    for q in (b, b + 1)
                ],
                axis=1,
            )
            rhs = jnp.concatenate([zcb[b, v], zcb[b + 1, v]], axis=0)
            moved = moved + dot_nn(lhs, rhs)
        zc = zbuf[z, v].astype(F32) - zmean[v]
        mask = jnp.where(std < 1.0, 1.0, 0.0)
        t = coef * (moved - zcb[z, v].astype(F32) * diag) - (hinge_coef * mask / std) * zc
        summed[v] = t
        local_sum.append(col_sum(t))
    gsum[z] = rows_of(local_sum, 256)
    totals = share_z(net, gsum)
    next(totals)
    diff = zbuf[z, 0].astype(F32) - zbuf[z, 1].astype(F32)
    inv_row = col_sum(diff * diff)
    wide = (25.0 / (ROWS * E)) * inv_row + (
        (25.0 / (2 * E)) * hinge_row - (1.0 / denom) * diag_row
    ) / PLANES
    share = wide[:, 0:128] + wide[:, 128:256] + (1.0 / denom) * ksq
    lsend[0] = rows_of([share], 128)
    loss_core = net.push(lsend.at[0], lrecv.at[0], net.partner())
    next(totals)
    for v in range(2):
        total = col_sum(gsum[:, v, :]) / ROWS
        sign = 1.0 if v == 0 else -1.0
        dz[z, v] = (summed[v] - total + (sign * inv_coef) * diff).astype(BF16).reshape(8, 16, 256)

    dring = ring_z(net, dz)
    next(dring)
    dzl = dz[z].reshape(256, 256)

    def dact_loop(store, parity):
        def step(i, carry):
            rows = w[pl.ds(pl.multiple_of((2 * i + parity) * 128, 128), 128), :]
            store[:, :, lax.div(i, 4), lax.rem(i, 4)] = dot_nt(dzl, rows).reshape(2, 2, 64, 128)
            return carry

        lax.fori_loop(0, 16, step, 0)

    dact_loop(dgive, 1 - core)
    over = [net.push(dgive.at[h], drecv.at[h], net.partner()) for h in range(2)]
    dact_loop(dkeep, core)
    for h in range(2):
        over[h].wait_recv()
        dpart[h] = (dkeep[h] + drecv[h]).astype(BF16)
    rs = reduce_plane(net, dpart, dtie1, dfull1, dmid, dtie2, dfull2, dact)
    next(rs)
    loss_core.wait_recv()
    lsend[1] = lsend[0] + lrecv[0]
    loss_x = [net.push(lsend.at[1], lrecv.at[d], net.at(y, mod4(x + d))) for d in range(1, 4)]
    next(dring)
    next(rs)
    next(dring)
    for copy in loss_x:
        copy.wait_recv()
    lsend[2] = lsend[1] + lrecv[1] + lrecv[2] + lrecv[3]
    loss_y = [net.push(lsend.at[2], lrecv.at[3 + d], net.at(mod4(y + d), x)) for d in range(1, 4)]
    next(rs)
    next(dring)
    next(rs)
    next(rs)
    for copy in loss_y:
        copy.wait_recv()
    plane_loss = lsend[2] + lrecv[4] + lrecv[5] + lrecv[6]

    sums = []
    for v in range(2):
        dp = dact[v].reshape(128, 128) * slope[v]
        dact[v] = dp.reshape(2, 64, 128)
        sums.append((col_sum(dp), col_sum(dp * xhat[v])))
    fstat[z] = rows_of([sums[0][0], sums[1][0], sums[0][1], sums[1][1], plane_loss[0:1]], 128)
    final = share_z(net, fstat)
    next(final)
    next(dring)

    def gw_step(i, carry):
        lhs, rhs = [], []
        for k in range(2):
            c = 2 * i + k
            cy, cx = lax.div(c, 4), lax.rem(c, 4)
            lhs.append(
                jnp.concatenate(
                    [act_t[cy, cx, q // 2, q % 2].reshape(128, 128) for q in range(4)], axis=1
                )
            )
            rhs.append(dz[:, lax.div(c, 8), lax.rem(c, 8)].reshape(128, 256))
        term = dot_tn(jnp.concatenate(lhs, axis=0), jnp.concatenate(rhs, axis=0))
        grad_weight[...] = jnp.where(i == 0, term, grad_weight[...] + term)
        return carry

    grad_weight[...] = jnp.zeros_like(grad_weight)
    lax.fori_loop(0, 8, gw_step, 0)
    next(final)
    total_b = [col_sum(fstat[:, v, :]) for v in range(2)]
    total_g = [col_sum(fstat[:, 2 + v, :]) for v in range(2)]
    grad_bias[...] = total_b[0] + total_b[1]
    grad_gain[...] = total_g[0] + total_g[1]
    loss[0, 0] = jnp.sum(fstat[:, 4, :])
    for v in range(2):
        dp = dact[v].reshape(128, 128)
        views_gradient[v] = (gain[...] * inverse[v]) * (
            dp - total_b[v] / ROWS - xhat[v] * (total_g[v] / ROWS)
        )
    for copy in net.sent:
        copy.wait_send()


MESSAGES = 280


def shards(views, norm_scale_gain, norm_shift_bias, weight):
    vmem = pltpu.VMEM

    def reducer(n, dtype):
        return [
            vmem((2, 2, 2, 2, n, 128), dtype),
            vmem((2, 2, 2, 4, n, 128), dtype),
            vmem((2, 2, 4, n, 128), F32),
            vmem((2, 2, n, 128), F32),
            vmem((2, 2, 2, n, 128), F32),
            vmem((2, 2, n, 128), F32),
        ]

    scratch = [
        vmem((4096, 256), BF16),
        vmem((4, 4, 2, 2, 2, 4, 16, 128), BF16),
        vmem((4, 4, 2, 2, 2, 4, 16, 128), BF16),
        vmem((2, 128, 128), F32),
        vmem((2, 128, 128), F32),
        vmem((8, 8, 128), F32),
        vmem((256, 256), F32),
        vmem((8, 2, 128, 256), BF16),
        vmem((8, 8, 256), F32),
        vmem((8, 2, 128, 256), BF16),
        vmem((8, 256), F32),
        vmem((2, 2, 2, 4, 4, 16, 128), F32),
        vmem((2, 2, 4, 4, 16, 128), F32),
        *reducer(16, F32),
        vmem((4, 4, 2, 2, 2, 16, 128), BF16),
        vmem((2, 128, 256), F32),
        vmem((8, 8, 256), F32),
        vmem((8, 2, 8, 16, 256), BF16),
        vmem((2, 2, 4, 4, 64, 128), F32),
        vmem((2, 2, 4, 4, 64, 128), F32),
        vmem((2, 2, 4, 4, 64, 128), F32),
        vmem((2, 2, 4, 4, 64, 128), BF16),
        *reducer(64, BF16),
        vmem((3, 8, 128), F32),
        vmem((7, 8, 128), F32),
        vmem((8, 8, 128), F32),
        pltpu.SemaphoreType.DMA((MESSAGES,)),
        pltpu.SemaphoreType.DMA((MESSAGES,)),
        pltpu.SemaphoreType.DMA,
    ]
    whole = pl.BlockSpec(memory_space=pltpu.VMEM)
    loss, grad_weight, grad_gain, grad_bias, views_gradient = pl.pallas_call(
        body,
        out_shape=(
            jax.ShapeDtypeStruct((1, 1), F32),
            jax.ShapeDtypeStruct((512, 256), F32),
            jax.ShapeDtypeStruct((1, 128), F32),
            jax.ShapeDtypeStruct((1, 128), F32),
            jax.ShapeDtypeStruct((2, 128, 128), F32),
        ),
        in_specs=[whole, whole, whole, pl.BlockSpec(memory_space=pl.ANY)],
        out_specs=(pl.BlockSpec(memory_space=pltpu.SMEM), whole, whole, whole, whole),
        scratch_shapes=scratch,
        compiler_params=pltpu.CompilerParams(collective_id=0, has_side_effects=True),
        name="vicreg_step",
    )(views, norm_scale_gain.reshape(1, 128), norm_shift_bias.reshape(1, 128), weight)
    return (
        loss.reshape(()),
        grad_weight,
        grad_gain.reshape(128),
        grad_bias.reshape(128),
        views_gradient,
    )


def solution(mesh):
    placed = (P(None, "batch", "col"), P("col"), P("col"), P(None, "col"))
    return jax.shard_map(
        shards,
        mesh=mesh,
        in_specs=placed,
        out_specs=(P(), P("batch", "col"), P("col"), P("col"), P(None, "batch", "col")),
        check_vma=False,
    )
```

```python
import jax
import jax.numpy as jnp
from jax import lax
from jax.experimental import pallas as pl
from jax.experimental.pallas import tpu as pltpu
from jax.sharding import PartitionSpec as P

E = 8192
ROWS = 1024
PLANES = 8
SIDE = 4

eps_norm = 1e-05
eps_std = 0.0001
scale = ROWS * E / 128.0
denom = float((ROWS - 1) ** 2 * E)
coef = 4.0 * scale / denom
hinge_coef = 25.0 * scale / (2.0 * E * (ROWS - 1))
inv_coef = 50.0 * scale / (ROWS * E)

F32 = jnp.float32
BF16 = jnp.bfloat16
MESH = pl.DeviceIdType.MESH


def dot_nt(a, b):
    return lax.dot_general(a, b, (((1,), (1,)), ((), ())), preferred_element_type=F32)


def dot_tn(a, b):
    return lax.dot_general(a, b, (((0,), (0,)), ((), ())), preferred_element_type=F32)


def dot_nn(a, b):
    return jnp.dot(a, b, preferred_element_type=F32)


class Net:
    def __init__(self, send, recv):
        self.send, self.recv, self.used, self.open = send, recv, 0, []
        self.z = lax.axis_index("batch")
        self.c = lax.axis_index("col")
        self.core = lax.rem(self.c, 2)
        self.chip = lax.div(self.c, 2)
        self.x = lax.rem(self.chip, SIDE)
        self.y = lax.div(self.chip, SIDE)

    def at_z(self, d):
        return (mod8(self.z + d), self.c)

    def at(self, y, x):
        return (self.z, (y * SIDE + x) * 2 + self.core)

    def along(self, h, f, t):
        return self.at(t, f) if h == 0 else self.at(f, t)

    def partner(self):
        return (self.z, self.chip * 2 + 1 - self.core)

    def copy(self, src, dst, device, i):
        return pltpu.make_async_remote_copy(
            src_ref=src,
            dst_ref=dst,
            send_sem=self.send.at[i],
            recv_sem=self.recv.at[i],
            device_id=device,
            device_id_type=MESH,
        )

    def group(self, meter):
        i = self.used
        self.used += 1
        whole = self.copy(meter, meter, self.partner(), i)
        self.open.append(whole)
        return i, whole

    def push(self, src, dst, device, group=None):
        if group is not None:
            self.copy(src, dst, device, group[0]).start()
            return None
        i = self.used
        self.used += 1
        one = self.copy(src, dst, device, i)
        one.start()
        self.open.append(one)
        return one

    def peers(self):
        found = [self.partner()]
        found += [self.at_z(d) for d in range(1, PLANES)]
        found += [self.at(mod4(self.y + dy), mod4(self.x + dx)) for dy, dx in OFFSETS]
        return found


OFFSETS = [(dy, dx) for dy in (2, 1, 3, 0) for dx in (2, 1, 3, 0) if (dy, dx) != (0, 0)]


def mod4(a):
    return lax.rem(a, SIDE)


def mod8(a):
    return lax.rem(a, PLANES)


def share_z(net, buf):
    group = net.group(buf.at[0:7])
    for d in (4, 3, 5, 2, 6, 1, 7):
        net.push(buf.at[net.z], buf.at[net.z], net.at_z(d), group)
    yield
    group[1].wait_recv()
    yield


def share_plane(net, src, dst):
    group = net.group(dst)
    for k, (dy, dx) in enumerate(OFFSETS):
        net.push(src, dst.at[k], net.at(mod4(net.y + dy), mod4(net.x + dx)), group)
    return group[1]


def ring_z(net, buf):
    up, down = {}, {}
    for q in range(4):
        own = buf.at[net.z, q]
        up[1, q] = net.push(own, own, net.at_z(1))
        down[1, q] = net.push(own, own, net.at_z(7))
    yield
    for d in range(1, 5):
        for q in range(4):
            if d < 4 or q < 2:
                up[d, q].wait_recv()
                if d < 3 or (d == 3 and q < 2):
                    block = buf.at[mod8(net.z + 8 - d), q]
                    up[d + 1, q] = net.push(block, block, net.at_z(1))
            if d < 4 or q >= 2:
                down[d, q].wait_recv()
                if d < 3 or (d == 3 and q >= 2):
                    block = buf.at[mod8(net.z + d), q]
                    down[d + 1, q] = net.push(block, block, net.at_z(7))
            if q == 1 and d < 4:
                yield
        yield


def gather_plane(net, buf):
    first_at, then_at = (net.x, net.y), (net.y, net.x)
    shift = (0, 3, 1, 2)
    first, cross, over = {}, {}, {}

    def piece(h, f, t):
        y, x = (t, f) if h == 0 else (f, t)
        return buf.at[y, x, net.core, h]

    def spread(h, j):
        f = mod4(first_at[h] + shift[j])
        cross[h, j] = net.group(buf.at[0:3, 0, 0, 0])
        block = piece(h, f, then_at[h])
        for d in (2, 1, 3):
            net.push(block, block, net.along(h, f_own[h], mod4(then_at[h] + d)), cross[h, j])

    def hand_over(h, j):
        cross[h, j][1].wait_recv()
        f = mod4(first_at[h] + shift[j])
        line = buf.at[:, f, net.core, 0] if h == 0 else buf.at[f, :, net.core, 1]
        over[h, j] = net.push(line, line, net.partner())

    f_own = first_at
    for h in range(2):
        block = piece(h, first_at[h], then_at[h])
        for d in (1, 3, 2):
            first[h, d] = net.push(block, block, net.along(h, mod4(first_at[h] + d), then_at[h]))
    for h in range(2):
        spread(h, 0)
    yield
    for j, d in ((1, 1), (2, 3), (3, 2)):
        for h in range(2):
            first[h, d].wait_recv()
            spread(h, j)
    yield
    for j in range(4):
        for h in range(2):
            hand_over(h, j)
        yield
        if j > 0:
            for h in range(2):
                over[h, j - 1].wait_recv()
            yield
    for h in range(2):
        over[h, 3].wait_recv()
    yield


def rows_of(parts, width):
    count = len(parts)
    rows = list(parts)
    if count < 8:
        rows.append(jnp.zeros((8 - count, width), F32))
    return jnp.concatenate(rows, axis=0)


def col_sum(t):
    return jnp.sum(t, axis=0, keepdims=True)


def split3(t):
    hi = t.astype(BF16)
    rest = t - hi.astype(F32)
    mid = rest.astype(BF16)
    lo = (rest - mid.astype(F32)).astype(BF16)
    zero = jnp.zeros((5, t.shape[1]), F32)
    return jnp.concatenate([hi.astype(F32), mid.astype(F32), lo.astype(F32), zero], axis=0).astype(BF16)


STAGES = ((1, 7), (2, 6), (3, 5), (0, 4))


def body(
    views,
    gain,
    bias,
    w_hbm,
    grad_weight,
    small,
    views_gradient,
    w,
    act,
    act_t,
    xhat,
    slope,
    stats,
    zacc,
    zbuf,
    zsum,
    zcb,
    colstat,
    kpart,
    krecv,
    kmine,
    kin,
    kown,
    kgat,
    rsum,
    rcore,
    rmine,
    rin,
    moved,
    dz,
    dgive,
    dkeep,
    drecv,
    dpart,
    din,
    dmid,
    dmid_in,
    dpre,
    lsend,
    lrecv,
    fstat,
    send_sems,
    recv_sems,
    load_sem,
):
    net = Net(send_sems, recv_sems)
    z, y, x, core, chip = net.z, net.y, net.x, net.core, net.chip
    load = pltpu.make_async_copy(w_hbm, w, load_sem)
    load.start()
    barrier = pltpu.get_barrier_semaphore()
    peers = net.peers()
    for peer in peers:
        pl.semaphore_signal(barrier, inc=1, device_id=peer, device_id_type=MESH)
    local = []
    for v in range(2):
        t = views[v].astype(F32)
        m = col_sum(t) / 128.0
        local.append((m, col_sum((t - m) * (t - m))))
    stats[z] = rows_of([local[0][0], local[1][0], local[0][1], local[1][1]], 128)
    pl.semaphore_wait(barrier, len(peers))

    g = share_z(net, stats)
    next(g)
    next(g)
    inverse = []
    for v in range(2):
        m = stats[:, v, :]
        mean = col_sum(m) / PLANES
        spread = col_sum(stats[:, 2 + v, :] + 128.0 * (m - mean) * (m - mean))
        inv = 1.0 / jnp.sqrt(spread / ROWS + eps_norm)
        inverse.append(inv)
        xh = (views[v].astype(F32) - mean) * inv
        pre = gain[...] * xh + bias[...]
        inner = 0.7978845608028654 * (pre + 0.044715 * (pre * pre * pre))
        th = jnp.tanh(inner)
        a = 0.5 * pre * (1.0 + th)
        act[y, x, core, v] = a.astype(BF16).reshape(2, 4, 16, 128)
        xhat[v] = xh
        slope[v] = 0.5 * (1.0 + th) + 0.5 * pre * (1.0 - th * th) * (
            0.7978845608028654 * (1.0 + 3.0 * 0.044715 * (pre * pre))
        )

    def z_terms(j):
        for h in range(2):
            if h == 0:
                f = mod4(x + (0, 3, 1, 2)[j])
                lhs = [act[k, f, q, 0].reshape(128, 128) for k in range(4) for q in range(2)]
                rhs = w[:, f].reshape(1024, 256)
            else:
                f = mod4(y + (0, 3, 1, 2)[j])
                lhs = [act[f, k, q, 1].reshape(128, 128) for k in range(4) for q in range(2)]
                rhs = w[f].reshape(1024, 256)
            term = dot_nn(jnp.concatenate(lhs, axis=1), rhs)
            if j == 0:
                zacc[h] = term
            else:
                zacc[h] = zacc[h] + term

    ag = gather_plane(net, act)
    next(ag)
    next(ag)
    next(ag)
    load.wait()
    for j in range(3):
        next(ag)
        next(ag)
        z_terms(j)
    next(ag)

    row_v, row_s, row_q = lax.div(chip, 8), lax.rem(lax.div(chip, 4), 2), lax.rem(chip, 4)

    def feature_rows(plane):
        owner = plane * 2 + core
        return act.at[lax.div(owner, 4), lax.rem(owner, 4), :, row_v, row_s, row_q]

    z_terms(3)
    zb = zacc[...].astype(BF16)
    zbuf[z] = zb.reshape(4, 64, 256)
    zf = zb.astype(F32)
    zsum[z] = rows_of([col_sum(zf[0]), col_sum(zf[1])], 256)
    means = share_z(net, zsum)
    next(means)
    zring = ring_z(net, zbuf)
    next(zring)
    own_rows = act_t.at[y, x, core, :, lax.div(z, 4), lax.rem(z, 4)]
    features = [
        net.push(feature_rows(mod8(z + d)), own_rows, net.at_z(d)) for d in range(1, PLANES)
    ]
    own_rows[...] = feature_rows(z)[...]
    colstat[...] = jnp.zeros_like(colstat)

    def block_in(stage, owner, v):
        slot = mod8(z + STAGES[stage][owner])
        zc = zbuf[slot, 2 * v : 2 * v + 2].reshape(128, 256).astype(F32) - zmean[v]
        cb = zc.astype(BF16)
        zcb[slot, v] = cb
        cf = cb.astype(F32)
        colstat[v : v + 1, :] += col_sum(zc * zc)
        colstat[2 + v : 3 + v, :] += col_sum(cf * cf)
        colstat[4 + v : 5 + v, :] += col_sum(cf)
        colstat[6 + v : 7 + v, :] += col_sum(zc)
        kpart[stage, owner, 8 * v : 8 * v + 8] = dot_nt(zcb[z, v], cb).reshape(8, 16, 128)

    k_over, k_in, k_gat, k_done = {}, {}, {}, {}

    def k_give(stage):
        k_over[stage] = net.push(kpart.at[stage, 1 - core], krecv.at[stage], net.partner())

    def k_spread(stage):
        k_over[stage].wait_recv()
        kmine[stage] = kpart[stage, core] + krecv[stage]
        group = net.group(kin.at[stage])
        for k, (dy, dx) in enumerate(OFFSETS):
            ty, tx = mod4(y + dy), mod4(x + dx)
            net.push(kmine.at[stage, ty * SIDE + tx], kin.at[stage, k], net.at(ty, tx), group)
        k_in[stage] = group[1]

    def k_gather(stage):
        k_in[stage].wait_recv()
        total = kmine[stage, chip] + jnp.sum(kin[stage], axis=0)
        kown[stage] = total
        kgat[stage, core, chip] = total.astype(BF16)
        own = kgat.at[stage, core, chip]
        group = net.group(kgat.at[stage, core, 0:15])
        for dy, dx in OFFSETS:
            net.push(own, own, net.at(mod4(y + dy), mod4(x + dx)), group)
        k_gat[stage] = group[1]

    def k_hand(stage):
        k_gat[stage].wait_recv()
        k_done[stage] = net.push(kgat.at[stage, core], kgat.at[stage, core], net.partner())

    def k_moved(stage):
        k_done[stage].wait_recv()
        slots = [mod8(z + r) for r in STAGES[stage]]
        for v in range(2):
            lhs = jnp.concatenate(
                [kgat[stage, q, 8 * v : 8 * v + 8].reshape(128, 128) for q in range(2)], axis=1
            )
            rhs = jnp.concatenate([zcb[slots[0], v], zcb[slots[1], v]], axis=0)
            term = dot_nn(lhs, rhs)
            if stage == 0:
                moved[v] = term
            else:
                moved[v] = moved[v] + term

    next(zring)
    for copy in features:
        copy.wait_recv()
    agt = gather_plane(net, act_t)
    next(agt)
    next(zring)
    next(means)
    zmean = [col_sum(zsum[:, v, :]) / ROWS for v in range(2)]
    for v in range(2):
        block_in(3, 0, v)
    for v in range(2):
        block_in(0, 0, v)
        block_in(0, 1, v)
    k_give(0)
    next(zring)
    k_spread(0)
    next(agt)
    next(zring)
    for v in range(2):
        block_in(1, 0, v)
        block_in(1, 1, v)
    k_give(1)
    next(zring)
    k_gather(0)
    k_spread(1)
    next(zring)
    for v in range(2):
        block_in(2, 0, v)
        block_in(2, 1, v)
    k_give(2)
    next(zring)
    for v in range(2):
        block_in(3, 1, v)
    k_give(3)
    k_spread(2)

    total_rows = [split3(colstat[4 + v : 5 + v, :]) for v in range(2)]
    for v in range(2):
        for slot in range(PLANES):
            rsum[v * PLANES + slot : v * PLANES + slot + 1, :] = col_sum(
                dot_nt(total_rows[v], zcb[slot, v])
            )
    r_over = net.push(rsum, rcore, net.partner())
    k_spread(3)
    k_gather(1)
    r_over.wait_recv()
    rmine[...] = rsum[...] + rcore[...]
    r_in = share_plane(net, rmine, rin)
    k_gather(2)
    k_hand(0)
    next(agt)
    k_gather(3)
    k_hand(1)
    k_moved(0)
    k_hand(2)
    k_moved(1)
    r_in.wait_recv()
    row_total = rmine[...] + jnp.sum(rin[...], axis=0)
    k_hand(3)
    k_moved(2)
    next(agt)
    next(agt)
    next(agt)
    next(agt)
    next(agt)
    next(agt)
    std, diag, mean_t = [], [], []
    for v in range(2):
        std.append(jnp.sqrt(colstat[v : v + 1, :] / (ROWS - 1) + eps_std))
        diag.append(colstat[2 + v : 3 + v, :])
        m = jnp.zeros((8, 256), F32)
        for slot in range(PLANES):
            r = v * PLANES + slot
            m = m + dot_nn(split3(row_total[r : r + 1, :]), zcb[slot, v])
        hinge = jnp.where(std[v] < 1.0, hinge_coef, 0.0) / std[v]
        mean_t.append(
            (
                coef * (col_sum(m) - diag[v] * colstat[4 + v : 5 + v, :])
                - hinge * colstat[6 + v : 7 + v, :]
            )
            / ROWS
        )
    k_moved(3)
    zl = [zbuf[z, 2 * v : 2 * v + 2].reshape(128, 256).astype(F32) for v in range(2)]
    diff = zl[0] - zl[1]
    for v in range(2):
        hinge = jnp.where(std[v] < 1.0, hinge_coef, 0.0) / std[v]
        t = coef * (moved[v] - zcb[z, v].astype(F32) * diag[v]) - hinge * (zl[v] - zmean[v])
        sign = 1.0 if v == 0 else -1.0
        d = (t - mean_t[v] + (sign * inv_coef) * diff).astype(BF16)
        dz[z, 2 * v : 2 * v + 2] = d.reshape(2, 4, 16, 256)

    dring = ring_z(net, dz)
    next(dring)
    first_at, then_at = (x, y), (y, x)
    dzl = [dz[z, 2 * v : 2 * v + 2].reshape(128, 256) for v in range(2)]
    d_over, d_in, d_mid = {}, {}, {}

    def d_terms(h, g, parity, store):
        f = mod4(first_at[h] + g)
        rows = w[:, f, parity] if h == 0 else w[f, :, parity]
        t = dot_nt(dzl[h], rows.reshape(512, 256))
        for k in range(4):
            store[h, g, k] = t[:, 128 * k : 128 * k + 128]

    def d_send(h, g):
        d_over[h, g].wait_recv()
        if g == 0:
            return
        dpart[h, g] = (dkeep[h, g] + drecv[h, g]).astype(BF16)
        f = mod4(first_at[h] + g)
        d_in[h, g] = net.push(dpart.at[h, g], din.at[h, g], net.along(h, f, then_at[h]))

    last = None
    for g in (2, 1, 3, 0):
        for h in range(2):
            d_terms(h, g, 1 - core, dgive)
            d_over[h, g] = net.push(dgive.at[h, g], drecv.at[h, g], net.partner())
        for h in range(2):
            d_terms(h, g, core, dkeep)
        if last is not None:
            for h in range(2):
                d_send(h, last)
        last = g
    next(dring)
    for h in range(2):
        d_send(h, 0)

    inv_row = col_sum(diff * diff)
    hinge_row = jnp.maximum(1.0 - std[0], 0.0) + jnp.maximum(1.0 - std[1], 0.0)
    diag_row = diag[0] * diag[0] + diag[1] * diag[1]
    wide = (25.0 / (ROWS * E)) * inv_row + (
        (25.0 / (2 * E)) * hinge_row - (1.0 / denom) * diag_row
    ) / PLANES
    ksq = col_sum(jnp.sum(kown[...] * kown[...], axis=0))
    share = wide[:, 0:128] + wide[:, 128:256] + (1.0 / denom) * ksq
    lsend[0] = rows_of([share], 128)
    loss_core = net.push(lsend.at[0], lrecv.at[15], net.partner())
    next(dring)
    next(dring)
    loss_core.wait_recv()
    lsend[1] = lsend[0] + lrecv[15]
    loss_in = share_plane(net, lsend.at[1], lrecv.at[0:15])
    for h in range(2):
        for g in range(1, 4):
            d_in[h, g].wait_recv()
        dmid[h] = dkeep[h, 0] + drecv[h, 0] + (
            din[h, 1].astype(F32) + din[h, 2].astype(F32) + din[h, 3].astype(F32)
        )
        group = net.group(dmid_in.at[h])
        for k, d in enumerate((2, 1, 3)):
            t = mod4(then_at[h] + d)
            net.push(dmid.at[h, t], dmid_in.at[h, k], net.along(h, first_at[h], t), group)
        d_mid[h] = group[1]
    next(dring)
    next(dring)
    loss_in.wait_recv()
    plane_loss = lsend[1, 0:1, :] + jnp.sum(lrecv[0:15, 0:1, :], axis=0)
    next(dring)
    sums = []
    for h in range(2):
        d_mid[h].wait_recv()
        d_act = dmid[h, then_at[h]] + dmid_in[h, 0] + dmid_in[h, 1] + dmid_in[h, 2]
        dp = d_act * slope[h]
        dpre[h] = dp
        sums.append((col_sum(dp), col_sum(dp * xhat[h])))
    fstat[z] = rows_of([sums[0][0], sums[1][0], sums[0][1], sums[1][1], plane_loss], 128)
    final = share_z(net, fstat)
    next(final)
    next(dring)
    next(agt)

    def gw_step(i, carry):
        lhs, rhs = [], []
        for k in range(2):
            c = 2 * i + k
            cy, cx = lax.div(c, 4), lax.rem(c, 4)
            lhs.append(
                jnp.concatenate(
                    [act_t[cy, cx, q // 2, q % 2].reshape(128, 128) for q in range(4)], axis=1
                )
            )
            rhs.append(dz[:, cy, cx].reshape(128, 256))
        term = dot_tn(jnp.concatenate(lhs, axis=0), jnp.concatenate(rhs, axis=0))
        grad_weight[...] = jnp.where(i == 0, term, grad_weight[...] + term)
        return carry

    grad_weight[...] = jnp.zeros_like(grad_weight)
    lax.fori_loop(0, 8, gw_step, 0)
    next(final)
    total_b = [col_sum(fstat[:, v, :]) for v in range(2)]
    total_g = [col_sum(fstat[:, 2 + v, :]) for v in range(2)]
    small[...] = rows_of([total_g[0] + total_g[1], total_b[0] + total_b[1], col_sum(fstat[:, 4, :])], 128)
    for v in range(2):
        views_gradient[v] = (gain[...] * inverse[v]) * (
            dpre[v] - total_b[v] / ROWS - xhat[v] * (total_g[v] / ROWS)
        )
    for copy in net.open:
        copy.wait_send()


MESSAGES = 150


def finish(gw_in, small, vg_in, loss, grad_weight, grad_gain, grad_bias, views_gradient):
    grad_weight[...] = gw_in[...]
    views_gradient[...] = vg_in[...]
    grad_gain[...] = small[0:1, :]
    grad_bias[...] = small[1:2, :]
    loss[0, 0] = jnp.sum(small[2:3, :])


def shards(views, norm_scale_gain, norm_shift_bias, weight):
    vmem = pltpu.VMEM
    scratch = [
        vmem((4, 4, 2, 128, 256), BF16),
        vmem((4, 4, 2, 2, 2, 4, 16, 128), BF16),
        vmem((4, 4, 2, 2, 2, 4, 16, 128), BF16),
        vmem((2, 128, 128), F32),
        vmem((2, 128, 128), F32),
        vmem((8, 8, 128), F32),
        vmem((2, 128, 256), F32),
        vmem((8, 4, 64, 256), BF16),
        vmem((8, 8, 256), F32),
        vmem((8, 2, 128, 256), BF16),
        vmem((8, 256), F32),
        vmem((4, 2, 16, 16, 128), F32),
        vmem((4, 16, 16, 128), F32),
        vmem((4, 16, 16, 128), F32),
        vmem((4, 15, 16, 128), F32),
        vmem((4, 16, 128), F32),
        vmem((4, 2, 16, 16, 128), BF16),
        vmem((16, 128), F32),
        vmem((16, 128), F32),
        vmem((16, 128), F32),
        vmem((15, 16, 128), F32),
        vmem((2, 128, 256), F32),
        vmem((8, 4, 4, 16, 256), BF16),
        vmem((2, 4, 4, 128, 128), F32),
        vmem((2, 4, 4, 128, 128), F32),
        vmem((2, 4, 4, 128, 128), F32),
        vmem((2, 4, 4, 128, 128), BF16),
        vmem((2, 4, 4, 128, 128), BF16),
        vmem((2, 4, 128, 128), F32),
        vmem((2, 3, 128, 128), F32),
        vmem((2, 128, 128), F32),
        vmem((2, 8, 128), F32),
        vmem((16, 8, 128), F32),
        vmem((8, 8, 128), F32),
        pltpu.SemaphoreType.DMA((MESSAGES,)),
        pltpu.SemaphoreType.DMA((MESSAGES,)),
        pltpu.SemaphoreType.DMA,
    ]
    whole = pl.BlockSpec(memory_space=pltpu.VMEM)
    made = (
        jax.ShapeDtypeStruct((512, 256), F32),
        jax.ShapeDtypeStruct((8, 128), F32),
        jax.ShapeDtypeStruct((2, 128, 128), F32),
    )
    results = pl.pallas_call(
        body,
        out_shape=made,
        in_specs=[whole, whole, whole, pl.BlockSpec(memory_space=pl.ANY)],
        out_specs=(whole, whole, whole),
        scratch_shapes=scratch,
        compiler_params=pltpu.CompilerParams(collective_id=0, has_side_effects=True),
        name="vicreg_step",
    )(
        views,
        norm_scale_gain.reshape(1, 128),
        norm_shift_bias.reshape(1, 128),
        weight.reshape(4, 4, 2, 128, 256),
    )
    loss, grad_weight, grad_gain, grad_bias, views_gradient = pl.pallas_call(
        finish,
        out_shape=(
            jax.ShapeDtypeStruct((1, 1), F32),
            made[0],
            jax.ShapeDtypeStruct((1, 128), F32),
            jax.ShapeDtypeStruct((1, 128), F32),
            made[2],
        ),
        in_specs=[whole, whole, whole],
        out_specs=(pl.BlockSpec(memory_space=pltpu.SMEM), whole, whole, whole, whole),
        name="write_results",
    )(*results)
    return (
        loss.reshape(()),
        grad_weight,
        grad_gain.reshape(128),
        grad_bias.reshape(128),
        views_gradient,
    )


def solution(mesh):
    placed = (P(None, "batch", "col"), P("col"), P("col"), P(None, "col"))
    return jax.shard_map(
        shards,
        mesh=mesh,
        in_specs=placed,
        out_specs=(P(), P("batch", "col"), P("col"), P("col"), P(None, "batch", "col")),
        check_vma=False,
    )
```

```python
import jax
import jax.numpy as jnp
from jax import lax
from jax.experimental import pallas as pl
from jax.experimental.pallas import tpu as pltpu
from jax.sharding import PartitionSpec as P

E = 8192
ROWS = 1024
PLANES = 8
SIDE = 4

eps_norm = 1e-05
eps_std = 0.0001
scale = ROWS * E / 128.0
denom = float((ROWS - 1) ** 2 * E)
coef = 4.0 * scale / denom
hinge_coef = 25.0 * scale / (2.0 * E * (ROWS - 1))
inv_coef = 50.0 * scale / (ROWS * E)

F32 = jnp.float32
BF16 = jnp.bfloat16
MESH = pl.DeviceIdType.MESH


def dot_nt(a, b):
    return lax.dot_general(a, b, (((1,), (1,)), ((), ())), preferred_element_type=F32)


def dot_tn(a, b):
    return lax.dot_general(a, b, (((0,), (0,)), ((), ())), preferred_element_type=F32)


def dot_nn(a, b):
    return jnp.dot(a, b, preferred_element_type=F32)


class Net:
    def __init__(self, send, recv):
        self.send, self.recv, self.n_send, self.n_recv, self.open = send, recv, 0, 0, []
        self.z = lax.axis_index("batch")
        self.c = lax.axis_index("col")
        self.core = lax.rem(self.c, 2)
        self.chip = lax.div(self.c, 2)
        self.x = lax.rem(self.chip, SIDE)
        self.y = lax.div(self.chip, SIDE)

    def at_z(self, d):
        return (mod8(self.z + d), self.c)

    def at(self, y, x):
        return (self.z, (y * SIDE + x) * 2 + self.core)

    def along(self, h, f, t):
        return self.at(t, f) if h == 0 else self.at(f, t)

    def partner(self):
        return (self.z, self.chip * 2 + 1 - self.core)

    def copy(self, src, dst, device, send, recv):
        return pltpu.make_async_remote_copy(
            src_ref=src,
            dst_ref=dst,
            send_sem=self.send.at[send],
            recv_sem=self.recv.at[recv],
            device_id=device,
            device_id_type=MESH,
        )

    def sends(self, meter):
        i = self.n_send
        self.n_send += 1
        self.open.append(self.copy(meter, meter, self.partner(), i, 0))
        return i

    def group(self, meter, sends=None):
        send = self.sends(meter) if sends is None else sends
        i = self.n_recv
        self.n_recv += 1
        return send, i, self.copy(meter, meter, self.partner(), send, i)

    def push(self, src, dst, device, group=None, sends=None):
        if group is not None:
            self.copy(src, dst, device, group[0], group[1]).start()
            return None
        send = self.sends(src) if sends is None else sends
        i = self.n_recv
        self.n_recv += 1
        one = self.copy(src, dst, device, send, i)
        one.start()
        return one

    def peers(self):
        found = [self.partner()]
        found += [self.at_z(d) for d in range(1, PLANES)]
        found += [self.at(mod4(self.y + dy), mod4(self.x + dx)) for dy, dx in OFFSETS]
        return found


OFFSETS = [(dy, dx) for dy in (2, 1, 3, 0) for dx in (2, 1, 3, 0) if (dy, dx) != (0, 0)]


def mod4(a):
    return lax.rem(a, SIDE)


def mod8(a):
    return lax.rem(a, PLANES)


def share_z(net, buf):
    group = net.group(buf.at[0:7])
    for d in (4, 3, 5, 2, 6, 1, 7):
        net.push(buf.at[net.z], buf.at[net.z], net.at_z(d), group)
    yield
    group[2].wait_recv()
    yield


def share_plane(net, src, dst):
    group = net.group(dst)
    for k, (dy, dx) in enumerate(OFFSETS):
        net.push(src, dst.at[k], net.at(mod4(net.y + dy), mod4(net.x + dx)), group)
    return group[2]


def ring_z(net, buf):
    sends = net.sends(buf.at[0:7])
    up, down = {}, {}
    for q in range(4):
        own = buf.at[net.z, q]
        up[1, q] = net.push(own, own, net.at_z(1), sends=sends)
        down[1, q] = net.push(own, own, net.at_z(7), sends=sends)
    yield
    for d in range(1, 5):
        for q in range(4 if d < 4 else 2):
            up[d, q].wait_recv()
            if d < 3 or (d == 3 and q < 2):
                block = buf.at[mod8(net.z + 8 - d), q]
                up[d + 1, q] = net.push(block, block, net.at_z(1), sends=sends)
            q = q if d < 4 else q + 2
            down[d, q].wait_recv()
            if d < 3 or (d == 3 and q >= 2):
                block = buf.at[mod8(net.z + d), q]
                down[d + 1, q] = net.push(block, block, net.at_z(7), sends=sends)
            yield


def gather_plane(net, buf):
    first_at, then_at = (net.x, net.y), (net.y, net.x)
    shift = (0, 3, 1, 2)
    first, cross, over = {}, {}, {}
    first_sends = net.sends(buf.at[0:3, 0, 0])
    cross_sends = net.sends(buf.at[0:3, :, 0])
    over_sends = net.sends(buf.at[:, :, 0])

    def piece(h, f, t):
        y, x = (t, f) if h == 0 else (f, t)
        return buf.at[y, x, net.core, h]

    def spread(h, j):
        f = mod4(first_at[h] + shift[j])
        cross[h, j] = net.group(buf.at[0:3, 0, 0, 0], cross_sends)
        block = piece(h, f, then_at[h])
        for d in (2, 1, 3):
            net.push(block, block, net.along(h, f_own[h], mod4(then_at[h] + d)), cross[h, j])

    def hand_over(h, j):
        cross[h, j][2].wait_recv()
        f = mod4(first_at[h] + shift[j])
        line = buf.at[:, f, net.core, 0] if h == 0 else buf.at[f, :, net.core, 1]
        over[h, j] = net.push(line, line, net.partner(), sends=over_sends)

    f_own = first_at
    for h in range(2):
        block = piece(h, first_at[h], then_at[h])
        for d in (1, 3, 2):
            to = net.along(h, mod4(first_at[h] + d), then_at[h])
            first[h, d] = net.push(block, block, to, sends=first_sends)
    for h in range(2):
        spread(h, 0)
    yield
    for j, d in ((1, 1), (2, 3), (3, 2)):
        for h in range(2):
            first[h, d].wait_recv()
            spread(h, j)
    yield
    for j in range(4):
        for h in range(2):
            hand_over(h, j)
        yield
        if j > 0:
            for h in range(2):
                over[h, j - 1].wait_recv()
            yield
    for h in range(2):
        over[h, 3].wait_recv()
    yield


def rows_of(parts, width):
    count = len(parts)
    rows = list(parts)
    if count < 8:
        rows.append(jnp.zeros((8 - count, width), F32))
    return jnp.concatenate(rows, axis=0)


def col_sum(t):
    return jnp.sum(t, axis=0, keepdims=True)


def split3(t):
    hi = t.astype(BF16)
    rest = t - hi.astype(F32)
    mid = rest.astype(BF16)
    lo = (rest - mid.astype(F32)).astype(BF16)
    zero = jnp.zeros((5, t.shape[1]), F32)
    return jnp.concatenate([hi.astype(F32), mid.astype(F32), lo.astype(F32), zero], axis=0).astype(BF16)


STAGES = ((1, 7), (2, 6), (3, 5), (0, 4))


def body(
    views_hbm,
    gain_hbm,
    bias_hbm,
    w_hbm,
    gw_hbm,
    small,
    views_gradient,
    views,
    gain,
    bias,
    grad_weight,
    w,
    act,
    act_t,
    xhat,
    slope,
    stats,
    zacc,
    zbuf,
    zsum,
    zcb,
    colstat,
    kpart,
    krecv,
    kmine,
    kin,
    kown,
    kgat,
    rsum,
    rcore,
    rmine,
    rin,
    moved,
    dz,
    dgive,
    dkeep,
    drecv,
    dpart,
    din,
    dmid,
    dmid_in,
    dpre,
    lsend,
    lrecv,
    fstat,
    send_sems,
    recv_sems,
    load_sem,
):
    net = Net(send_sems, recv_sems)
    z, y, x, core, chip = net.z, net.y, net.x, net.core, net.chip
    load_views = pltpu.make_async_copy(views_hbm, views, load_sem.at[0])
    load_gain = pltpu.make_async_copy(gain_hbm, gain, load_sem.at[1])
    load_bias = pltpu.make_async_copy(bias_hbm, bias, load_sem.at[2])
    load = pltpu.make_async_copy(w_hbm, w, load_sem.at[3])
    load_views.start()
    barrier = pltpu.get_barrier_semaphore()
    peers = net.peers()
    for peer in peers:
        pl.semaphore_signal(barrier, inc=1, device_id=peer, device_id_type=MESH)
    load_gain.start()
    load_bias.start()
    load.start()
    load_views.wait()
    local = []
    for v in range(2):
        t = views[v].astype(F32)
        m = col_sum(t) / 128.0
        local.append((m, col_sum((t - m) * (t - m))))
    stats[z] = rows_of([local[0][0], local[1][0], local[0][1], local[1][1]], 128)
    pl.semaphore_wait(barrier, len(peers))

    g = share_z(net, stats)
    next(g)
    load_gain.wait()
    load_bias.wait()
    next(g)
    inverse = []
    for v in range(2):
        m = stats[:, v, :]
        mean = col_sum(m) / PLANES
        spread = col_sum(stats[:, 2 + v, :] + 128.0 * (m - mean) * (m - mean))
        inv = 1.0 / jnp.sqrt(spread / ROWS + eps_norm)
        inverse.append(inv)
        xh = (views[v].astype(F32) - mean) * inv
        pre = gain[...] * xh + bias[...]
        inner = 0.7978845608028654 * (pre + 0.044715 * (pre * pre * pre))
        th = jnp.tanh(inner)
        a = 0.5 * pre * (1.0 + th)
        act[y, x, core, v] = a.astype(BF16).reshape(2, 4, 16, 128)
        xhat[v] = xh
        slope[v] = 0.5 * (1.0 + th) + 0.5 * pre * (1.0 - th * th) * (
            0.7978845608028654 * (1.0 + 3.0 * 0.044715 * (pre * pre))
        )

    def z_terms(j):
        for h in range(2):
            if h == 0:
                f = mod4(x + (0, 3, 1, 2)[j])
                lhs = [act[k, f, q, 0].reshape(128, 128) for k in range(4) for q in range(2)]
                rhs = w[:, f].reshape(1024, 256)
            else:
                f = mod4(y + (0, 3, 1, 2)[j])
                lhs = [act[f, k, q, 1].reshape(128, 128) for k in range(4) for q in range(2)]
                rhs = w[f].reshape(1024, 256)
            term = dot_nn(jnp.concatenate(lhs, axis=1), rhs)
            if j == 0:
                zacc[h] = term
            else:
                zacc[h] = zacc[h] + term

    ag = gather_plane(net, act)
    next(ag)
    next(ag)
    next(ag)
    load.wait()
    for j in range(3):
        next(ag)
        next(ag)
        z_terms(j)
    next(ag)

    row_v, row_s, row_q = lax.div(chip, 8), lax.rem(lax.div(chip, 4), 2), lax.rem(chip, 4)

    def feature_rows(plane):
        owner = plane * 2 + core
        return act.at[lax.div(owner, 4), lax.rem(owner, 4), :, row_v, row_s, row_q]

    z_terms(3)
    zb = zacc[...].astype(BF16)
    zbuf[z] = zb.reshape(4, 64, 256)
    zf = zb.astype(F32)
    zsums = [col_sum(zf[v])[:, k : k + 128] for v in range(2) for k in (0, 128)]
    zsum[z] = jnp.concatenate(zsums, axis=0)
    means = share_z(net, zsum)
    next(means)
    own_rows = act_t.at[y, x, core, :, lax.div(z, 4), lax.rem(z, 4)]
    features = net.group(kgat.at[0, 0, 0:14])
    for d in (4, 3, 5, 2, 6, 1, 7):
        net.push(feature_rows(mod8(z + d)), own_rows, net.at_z(d), features)
    zring = ring_z(net, zbuf)
    next(zring)
    own_rows[...] = feature_rows(z)[...]
    colstat[...] = jnp.zeros_like(colstat)

    def block_in(stage, owner, v):
        slot = mod8(z + STAGES[stage][owner])
        zc = zbuf[slot, 2 * v : 2 * v + 2].reshape(128, 256).astype(F32) - zmean[v]
        cb = zc.astype(BF16)
        zcb[slot, v] = cb
        cf = cb.astype(F32)
        colstat[v : v + 1, :] += col_sum(zc * zc)
        colstat[2 + v : 3 + v, :] += col_sum(cf * cf)
        colstat[4 + v : 5 + v, :] += col_sum(cf)
        kpart[stage, owner, 8 * v : 8 * v + 8] = dot_nt(zcb[z, v], cb).reshape(8, 16, 128)

    k_over, k_in, k_gat, k_done = {}, {}, {}, {}
    k_sends = [
        net.sends(m) for m in (kpart.at[:, 0], kin, kgat.at[:, 0, 0:15], kgat.at[:, 0])
    ]

    def k_give(stage):
        k_over[stage] = net.push(
            kpart.at[stage, 1 - core], krecv.at[stage], net.partner(), sends=k_sends[0]
        )

    def k_spread(stage):
        k_over[stage].wait_recv()
        kmine[stage] = kpart[stage, core] + krecv[stage]
        group = net.group(kin.at[stage], k_sends[1])
        for k, (dy, dx) in enumerate(OFFSETS):
            ty, tx = mod4(y + dy), mod4(x + dx)
            net.push(kmine.at[stage, ty * SIDE + tx], kin.at[stage, k], net.at(ty, tx), group)
        k_in[stage] = group[2]

    def k_gather(stage):
        k_in[stage].wait_recv()
        total = kmine[stage, chip] + jnp.sum(kin[stage], axis=0)
        kown[stage] = total
        kgat[stage, core, chip] = total.astype(BF16)
        own = kgat.at[stage, core, chip]
        group = net.group(kgat.at[stage, core, 0:15], k_sends[2])
        for dy, dx in OFFSETS:
            net.push(own, own, net.at(mod4(y + dy), mod4(x + dx)), group)
        k_gat[stage] = group[2]

    def k_hand(stage):
        k_gat[stage].wait_recv()
        k_done[stage] = net.push(
            kgat.at[stage, core], kgat.at[stage, core], net.partner(), sends=k_sends[3]
        )

    def k_moved(stage):
        k_done[stage].wait_recv()
        slots = [mod8(z + r) for r in STAGES[stage]]
        for v in range(2):
            lhs = jnp.concatenate(
                [kgat[stage, q, 8 * v : 8 * v + 8].reshape(128, 128) for q in range(2)], axis=1
            )
            rhs = jnp.concatenate([zcb[slots[0], v], zcb[slots[1], v]], axis=0)
            term = dot_nn(lhs, rhs)
            if stage == 0:
                moved[v] = term
            else:
                moved[v] = moved[v] + term

    def step(count):
        for _ in range(count):
            next(zring)

    def blocks(stage):
        for v in range(2):
            block_in(stage, 0, v)
            block_in(stage, 1, v)

    step(6)
    next(means)
    ztotal = [
        jnp.concatenate([col_sum(zsum[:, 2 * v + k, :]) for k in range(2)], axis=1) for v in range(2)
    ]
    zmean = [t / ROWS for t in ztotal]
    block_in(3, 0, 0)
    block_in(3, 0, 1)
    blocks(0)
    k_give(0)
    features[2].wait_recv()
    agt = gather_plane(net, act_t)
    next(agt)
    step(2)
    blocks(1)
    k_give(1)
    k_spread(0)
    step(1)
    next(agt)
    step(2)
    k_spread(1)
    step(1)
    blocks(2)
    k_give(2)
    step(1)
    k_gather(0)
    step(1)
    block_in(3, 1, 0)
    block_in(3, 1, 1)
    k_give(3)
    k_spread(2)
    k_gather(1)
    k_spread(3)

    total_rows = [split3(colstat[4 + v : 5 + v, :]) for v in range(2)]
    for v in range(2):
        for slot in range(PLANES):
            rsum[v * PLANES + slot : v * PLANES + slot + 1, :] = col_sum(
                dot_nt(total_rows[v], zcb[slot, v])
            )
    r_over = net.push(rsum, rcore, net.partner())
    k_gather(2)
    k_hand(0)
    r_over.wait_recv()
    rmine[...] = rsum[...] + rcore[...]
    r_in = share_plane(net, rmine, rin)
    k_hand(1)
    next(agt)
    k_gather(3)
    k_moved(0)
    k_hand(2)
    k_moved(1)
    r_in.wait_recv()
    row_total = rmine[...] + jnp.sum(rin[...], axis=0)
    k_hand(3)
    k_moved(2)
    next(agt)
    next(agt)
    next(agt)
    next(agt)
    next(agt)
    next(agt)
    std, diag, mean_t = [], [], []
    for v in range(2):
        std.append(jnp.sqrt(colstat[v : v + 1, :] / (ROWS - 1) + eps_std))
        diag.append(colstat[2 + v : 3 + v, :])
        m = jnp.zeros((8, 256), F32)
        for slot in range(PLANES):
            r = v * PLANES + slot
            m = m + dot_nn(split3(row_total[r : r + 1, :]), zcb[slot, v])
        hinge = jnp.where(std[v] < 1.0, hinge_coef, 0.0) / std[v]
        mean_t.append(
            (
                coef * (col_sum(m) - diag[v] * colstat[4 + v : 5 + v, :])
                - hinge * (ztotal[v] - ROWS * zmean[v])
            )
            / ROWS
        )
    k_moved(3)
    zl = [zbuf[z, 2 * v : 2 * v + 2].reshape(128, 256).astype(F32) for v in range(2)]
    diff = zl[0] - zl[1]
    for v in range(2):
        hinge = jnp.where(std[v] < 1.0, hinge_coef, 0.0) / std[v]
        t = coef * (moved[v] - zcb[z, v].astype(F32) * diag[v]) - hinge * (zl[v] - zmean[v])
        sign = 1.0 if v == 0 else -1.0
        d = (t - mean_t[v] + (sign * inv_coef) * diff).astype(BF16)
        dz[z, 2 * v : 2 * v + 2] = d.reshape(2, 4, 16, 256)

    dring = ring_z(net, dz)
    next(dring)
    first_at, then_at = (x, y), (y, x)
    dzl = [dz[z, 2 * v : 2 * v + 2].reshape(128, 256) for v in range(2)]
    d_over, d_in, d_mid = {}, {}, {}
    d_sends = [net.sends(dgive), net.sends(dpart.at[:, 1:4])]

    def d_terms(h, g, parity, store):
        f = mod4(first_at[h] + g)
        rows = w[:, f, parity] if h == 0 else w[f, :, parity]
        t = dot_nt(dzl[h], rows.reshape(512, 256))
        for k in range(4):
            store[h, g, k] = t[:, 128 * k : 128 * k + 128]

    def d_send(h, g):
        d_over[h, g].wait_recv()
        if g == 0:
            return
        dpart[h, g] = (dkeep[h, g] + drecv[h, g]).astype(BF16)
        f = mod4(first_at[h] + g)
        to = net.along(h, f, then_at[h])
        d_in[h, g] = net.push(dpart.at[h, g], din.at[h, g], to, sends=d_sends[1])

    last = None
    for g in (2, 1, 3, 0):
        for h in range(2):
            d_terms(h, g, 1 - core, dgive)
            d_over[h, g] = net.push(
                dgive.at[h, g], drecv.at[h, g], net.partner(), sends=d_sends[0]
            )
        for h in range(2):
            d_terms(h, g, core, dkeep)
        if last is not None:
            for h in range(2):
                d_send(h, last)
        last = g
    next(dring)
    next(dring)
    for h in range(2):
        d_send(h, 0)
    next(dring)

    inv_row = col_sum(diff * diff)
    hinge_row = jnp.maximum(1.0 - std[0], 0.0) + jnp.maximum(1.0 - std[1], 0.0)
    diag_row = diag[0] * diag[0] + diag[1] * diag[1]
    wide = (25.0 / (ROWS * E)) * inv_row + (
        (25.0 / (2 * E)) * hinge_row - (1.0 / denom) * diag_row
    ) / PLANES
    ksq = col_sum(jnp.sum(kown[...] * kown[...], axis=0))
    share = wide[:, 0:128] + wide[:, 128:256] + (1.0 / denom) * ksq
    lsend[0] = rows_of([share], 128)
    loss_core = net.push(lsend.at[0], lrecv.at[15], net.partner())
    next(dring)
    next(dring)
    loss_core.wait_recv()
    lsend[1] = lsend[0] + lrecv[15]
    loss_in = share_plane(net, lsend.at[1], lrecv.at[0:15])
    next(dring)
    next(dring)
    next(dring)
    for h in range(2):
        for g in range(1, 4):
            d_in[h, g].wait_recv()
        dmid[h] = dkeep[h, 0] + drecv[h, 0] + (
            din[h, 1].astype(F32) + din[h, 2].astype(F32) + din[h, 3].astype(F32)
        )
        group = net.group(dmid_in.at[h])
        for k, d in enumerate((2, 1, 3)):
            t = mod4(then_at[h] + d)
            net.push(dmid.at[h, t], dmid_in.at[h, k], net.along(h, first_at[h], t), group)
        d_mid[h] = group[2]
    next(dring)
    next(dring)
    loss_in.wait_recv()
    plane_loss = lsend[1, 0:1, :] + jnp.sum(lrecv[0:15, 0:1, :], axis=0)
    next(dring)
    next(dring)
    sums = []
    for h in range(2):
        d_mid[h].wait_recv()
        d_act = dmid[h, then_at[h]] + dmid_in[h, 0] + dmid_in[h, 1] + dmid_in[h, 2]
        dp = d_act * slope[h]
        dpre[h] = dp
        sums.append((col_sum(dp), col_sum(dp * xhat[h])))
    fstat[z] = rows_of([sums[0][0], sums[1][0], sums[0][1], sums[1][1], plane_loss], 128)
    final = share_z(net, fstat)
    next(final)
    next(dring)
    next(dring)
    next(agt)

    def gw_step(i, carry):
        lhs, rhs = [], []
        for k in range(2):
            c = 2 * i + k
            cy, cx = lax.div(c, 4), lax.rem(c, 4)
            lhs.append(
                jnp.concatenate(
                    [act_t[cy, cx, q // 2, q % 2].reshape(128, 128) for q in range(4)], axis=1
                )
            )
            rhs.append(dz[:, cy, cx].reshape(128, 256))
        term = dot_tn(jnp.concatenate(lhs, axis=0), jnp.concatenate(rhs, axis=0))
        grad_weight[...] = jnp.where(i == 0, term, grad_weight[...] + term)
        return carry

    grad_weight[...] = jnp.zeros_like(grad_weight)
    lax.fori_loop(0, 8, gw_step, 0)
    put = pltpu.make_async_copy(grad_weight, gw_hbm, load_sem.at[4])
    put.start()
    next(final)
    total_b = [col_sum(fstat[:, v, :]) for v in range(2)]
    total_g = [col_sum(fstat[:, 2 + v, :]) for v in range(2)]
    small[...] = rows_of([total_g[0] + total_g[1], total_b[0] + total_b[1], col_sum(fstat[:, 4, :])], 128)
    for v in range(2):
        views_gradient[v] = (gain[...] * inverse[v]) * (
            dpre[v] - total_b[v] / ROWS - xhat[v] * (total_g[v] / ROWS)
        )
    put.wait()
    for copy in net.open:
        copy.wait_send()


SENDS = 24
RECEIVES = 140


def finish(gw_in, small, vg_in, loss, grad_weight, grad_gain, grad_bias, views_gradient):
    grad_weight[...] = gw_in[...]
    views_gradient[...] = vg_in[...]
    grad_gain[...] = small[0:1, :]
    grad_bias[...] = small[1:2, :]
    loss[0, 0] = jnp.sum(small[2:3, :])


def shards(views, norm_scale_gain, norm_shift_bias, weight):
    vmem = pltpu.VMEM
    scratch = [
        vmem((2, 128, 128), BF16),
        vmem((1, 128), F32),
        vmem((1, 128), F32),
        vmem((512, 256), F32),
        vmem((4, 4, 2, 128, 256), BF16),
        vmem((4, 4, 2, 2, 2, 4, 16, 128), BF16),
        vmem((4, 4, 2, 2, 2, 4, 16, 128), BF16),
        vmem((2, 128, 128), F32),
        vmem((2, 128, 128), F32),
        vmem((8, 8, 128), F32),
        vmem((2, 128, 256), F32),
        vmem((8, 4, 64, 256), BF16),
        vmem((8, 4, 128), F32),
        vmem((8, 2, 128, 256), BF16),
        vmem((8, 256), F32),
        vmem((4, 2, 16, 16, 128), F32),
        vmem((4, 16, 16, 128), F32),
        vmem((4, 16, 16, 128), F32),
        vmem((4, 15, 16, 128), F32),
        vmem((4, 16, 128), F32),
        vmem((4, 2, 16, 16, 128), BF16),
        vmem((16, 128), F32),
        vmem((16, 128), F32),
        vmem((16, 128), F32),
        vmem((15, 16, 128), F32),
        vmem((2, 128, 256), F32),
        vmem((8, 4, 4, 16, 256), BF16),
        vmem((2, 4, 4, 128, 128), F32),
        vmem((2, 4, 4, 128, 128), F32),
        vmem((2, 4, 4, 128, 128), F32),
        vmem((2, 4, 4, 128, 128), BF16),
        vmem((2, 4, 4, 128, 128), BF16),
        vmem((2, 4, 128, 128), F32),
        vmem((2, 3, 128, 128), F32),
        vmem((2, 128, 128), F32),
        vmem((2, 8, 128), F32),
        vmem((16, 8, 128), F32),
        vmem((8, 8, 128), F32),
        pltpu.SemaphoreType.DMA((SENDS,)),
        pltpu.SemaphoreType.DMA((RECEIVES,)),
        pltpu.SemaphoreType.DMA((5,)),
    ]
    whole = pl.BlockSpec(memory_space=pltpu.VMEM)
    made = (
        jax.ShapeDtypeStruct((512, 256), F32),
        jax.ShapeDtypeStruct((8, 128), F32),
        jax.ShapeDtypeStruct((2, 128, 128), F32),
    )
    results = pl.pallas_call(
        body,
        out_shape=made,
        in_specs=[pl.BlockSpec(memory_space=pl.ANY)] * 4,
        out_specs=(pl.BlockSpec(memory_space=pl.ANY), whole, whole),
        scratch_shapes=scratch,
        compiler_params=pltpu.CompilerParams(collective_id=0, has_side_effects=True),
        name="vicreg_step",
    )(
        views,
        norm_scale_gain.reshape(1, 128),
        norm_shift_bias.reshape(1, 128),
        weight.reshape(4, 4, 2, 128, 256),
    )
    loss, grad_weight, grad_gain, grad_bias, views_gradient = pl.pallas_call(
        finish,
        out_shape=(
            jax.ShapeDtypeStruct((1, 1), F32),
            made[0],
            jax.ShapeDtypeStruct((1, 128), F32),
            jax.ShapeDtypeStruct((1, 128), F32),
            made[2],
        ),
        in_specs=[whole, whole, whole],
        out_specs=(pl.BlockSpec(memory_space=pltpu.SMEM), whole, whole, whole, whole),
        name="write_results",
    )(*results)
    return (
        loss.reshape(()),
        grad_weight,
        grad_gain.reshape(128),
        grad_bias.reshape(128),
        views_gradient,
    )


def solution(mesh):
    placed = (P(None, "batch", "col"), P("col"), P("col"), P(None, "col"))
    return jax.shard_map(
        shards,
        mesh=mesh,
        in_specs=placed,
        out_specs=(P(), P("batch", "col"), P("col"), P("col"), P(None, "batch", "col")),
        check_vma=False,
    )
```

```python
import jax
import jax.numpy as jnp
from jax import lax
from jax.experimental import pallas as pl
from jax.experimental.pallas import tpu as pltpu
from jax.sharding import PartitionSpec as P

E = 8192
ROWS = 1024
PLANES = 8
SIDE = 4

eps_norm = 1e-05
eps_std = 0.0001
scale = ROWS * E / 128.0
denom = float((ROWS - 1) ** 2 * E)
coef = 4.0 * scale / denom
hinge_coef = 25.0 * scale / (2.0 * E * (ROWS - 1))
inv_coef = 50.0 * scale / (ROWS * E)

F32 = jnp.float32
BF16 = jnp.bfloat16
MESH = pl.DeviceIdType.MESH


def dot_nt(a, b):
    return lax.dot_general(a, b, (((1,), (1,)), ((), ())), preferred_element_type=F32)


def dot_tn(a, b):
    return lax.dot_general(a, b, (((0,), (0,)), ((), ())), preferred_element_type=F32)


def dot_nn(a, b):
    return jnp.dot(a, b, preferred_element_type=F32)


class Net:
    def __init__(self, send, recv):
        self.send, self.recv, self.n_send, self.n_recv, self.open = send, recv, 0, 0, []
        self.z = lax.axis_index("batch")
        self.c = lax.axis_index("col")
        self.core = lax.rem(self.c, 2)
        self.chip = lax.div(self.c, 2)
        self.x = lax.rem(self.chip, SIDE)
        self.y = lax.div(self.chip, SIDE)

    def at_z(self, d):
        return (mod8(self.z + d), self.c)

    def at(self, y, x):
        return (self.z, (y * SIDE + x) * 2 + self.core)

    def other(self, y, x):
        return (self.z, (y * SIDE + x) * 2 + 1 - self.core)

    def along(self, h, f, t):
        return self.at(t, f) if h == 0 else self.at(f, t)

    def partner(self):
        return (self.z, self.chip * 2 + 1 - self.core)

    def copy(self, src, dst, device, send, recv):
        return pltpu.make_async_remote_copy(
            src_ref=src,
            dst_ref=dst,
            send_sem=self.send.at[send],
            recv_sem=self.recv.at[recv],
            device_id=device,
            device_id_type=MESH,
        )

    def sends(self, meter):
        i = self.n_send
        self.n_send += 1
        self.open.append(self.copy(meter, meter, self.partner(), i, 0))
        return i

    def group(self, meter, sends=None):
        send = self.sends(meter) if sends is None else sends
        i = self.n_recv
        self.n_recv += 1
        return send, i, self.copy(meter, meter, self.partner(), send, i)

    def push(self, src, dst, device, group=None, sends=None):
        if group is not None:
            self.copy(src, dst, device, group[0], group[1]).start()
            return None
        send = self.sends(src) if sends is None else sends
        i = self.n_recv
        self.n_recv += 1
        one = self.copy(src, dst, device, send, i)
        one.start()
        return one

    def peers(self):
        found = [self.partner()]
        found += [self.at_z(d) for d in range(1, PLANES)]
        for dy, dx in OFFSETS:
            found.append(self.at(mod4(self.y + dy), mod4(self.x + dx)))
            found.append(self.other(mod4(self.y + dy), mod4(self.x + dx)))
        return found


OFFSETS = [(dy, dx) for dy in (2, 1, 3, 0) for dx in (2, 1, 3, 0) if (dy, dx) != (0, 0)]


def mod4(a):
    return lax.rem(a, SIDE)


def mod8(a):
    return lax.rem(a, PLANES)


def share_z(net, buf):
    group = net.group(buf.at[0:7])
    for d in (4, 3, 5, 2, 6, 1, 7):
        net.push(buf.at[net.z], buf.at[net.z], net.at_z(d), group)
    yield
    group[2].wait_recv()
    yield


def share_plane(net, src, dst):
    group = net.group(dst)
    for k, (dy, dx) in enumerate(OFFSETS):
        net.push(src, dst.at[k], net.at(mod4(net.y + dy), mod4(net.x + dx)), group)
    return group[2]


def ring_z(net, buf):
    sends = net.sends(buf.at[0:7])
    up, down = {}, {}
    for q in range(4):
        own = buf.at[net.z, q]
        up[1, q] = net.push(own, own, net.at_z(1), sends=sends)
        down[1, q] = net.push(own, own, net.at_z(7), sends=sends)
    yield
    for d in range(1, 5):
        for q in range(4 if d < 4 else 2):
            up[d, q].wait_recv()
            if d < 3 or (d == 3 and q < 2):
                block = buf.at[mod8(net.z + 8 - d), q]
                up[d + 1, q] = net.push(block, block, net.at_z(1), sends=sends)
            q = q if d < 4 else q + 2
            down[d, q].wait_recv()
            if d < 3 or (d == 3 and q >= 2):
                block = buf.at[mod8(net.z + d), q]
                down[d + 1, q] = net.push(block, block, net.at_z(7), sends=sends)
            yield


def gather_plane(net, buf, late=False):
    first_at, then_at = (net.x, net.y), (net.y, net.x)
    shift = (0, 3, 1, 2)
    first, cross, over = {}, {}, {}
    first_sends = net.sends(buf.at[0:3, 0, 0])
    cross_sends = net.sends(buf.at[0:3, :, 0])
    over_sends = net.sends(buf.at[:, :, 0])

    def piece(h, f, t):
        y, x = (t, f) if h == 0 else (f, t)
        return buf.at[y, x, net.core, h]

    def spread(h, j):
        f = mod4(first_at[h] + shift[j])
        cross[h, j] = net.group(buf.at[0:3, 0, 0, 0], cross_sends)
        block = piece(h, f, then_at[h])
        for d in (2, 1, 3):
            net.push(block, block, net.along(h, f_own[h], mod4(then_at[h] + d)), cross[h, j])

    def hand_over(h, j):
        cross[h, j][2].wait_recv()
        f = mod4(first_at[h] + shift[j])
        line = buf.at[:, f, net.core, 0] if h == 0 else buf.at[f, :, net.core, 1]
        over[h, j] = net.push(line, line, net.partner(), sends=over_sends)

    f_own = first_at
    for h in range(2):
        block = piece(h, first_at[h], then_at[h])
        for d in (1, 3, 2):
            to = net.along(h, mod4(first_at[h] + d), then_at[h])
            first[h, d] = net.push(block, block, to, sends=first_sends)
    for h in range(2):
        spread(h, 0)
    yield
    for j, d in ((1, 1), (2, 3), (3, 2)):
        for h in range(2):
            first[h, d].wait_recv()
            spread(h, j)
    yield
    if late:
        for j in range(4):
            for h in range(2):
                hand_over(h, j)
        yield
        for copy in over.values():
            copy.wait_recv()
        yield
        return
    for j in range(4):
        for h in range(2):
            hand_over(h, j)
        yield
        if j > 0:
            for h in range(2):
                over[h, j - 1].wait_recv()
            yield
    for h in range(2):
        over[h, 3].wait_recv()
    yield


def rows_of(parts, width):
    count = len(parts)
    rows = list(parts)
    if count < 8:
        rows.append(jnp.zeros((8 - count, width), F32))
    return jnp.concatenate(rows, axis=0)


def col_sum(t):
    return jnp.sum(t, axis=0, keepdims=True)


def split3(t):
    hi = t.astype(BF16)
    rest = t - hi.astype(F32)
    mid = rest.astype(BF16)
    lo = (rest - mid.astype(F32)).astype(BF16)
    zero = jnp.zeros((5, t.shape[1]), F32)
    return jnp.concatenate([hi.astype(F32), mid.astype(F32), lo.astype(F32), zero], axis=0).astype(BF16)


STAGES = ((1, 7), (2, 6), (3, 5), (0, 4))


def body(
    views_hbm,
    gain_hbm,
    bias_hbm,
    w_hbm,
    gw_hbm,
    small,
    views_gradient,
    views,
    gain,
    bias,
    grad_weight,
    w,
    act,
    act_t,
    xhat,
    slope,
    stats,
    zacc,
    zbuf,
    zsum,
    zcb,
    colstat,
    kpart,
    krecv,
    kmine,
    kin,
    kown,
    kgat,
    rsum,
    rcore,
    rmine,
    rin,
    moved,
    dz,
    dgive,
    dkeep,
    drecv,
    dpart,
    din,
    dmid,
    dmid_in,
    dpre,
    lsend,
    lrecv,
    fstat,
    send_sems,
    recv_sems,
    load_sem,
):
    net = Net(send_sems, recv_sems)
    z, y, x, core, chip = net.z, net.y, net.x, net.core, net.chip
    load_views = pltpu.make_async_copy(views_hbm, views, load_sem.at[0])
    load_gain = pltpu.make_async_copy(gain_hbm, gain, load_sem.at[1])
    load_bias = pltpu.make_async_copy(bias_hbm, bias, load_sem.at[2])
    load = pltpu.make_async_copy(w_hbm, w, load_sem.at[3])
    load_views.start()
    barrier = pltpu.get_barrier_semaphore()
    peers = net.peers()
    for peer in peers:
        pl.semaphore_signal(barrier, inc=1, device_id=peer, device_id_type=MESH)
    load_gain.start()
    load_bias.start()
    load.start()
    load_views.wait()
    local = []
    for v in range(2):
        t = views[v].astype(F32)
        m = col_sum(t) / 128.0
        local.append((m, col_sum((t - m) * (t - m))))
    stats[z] = rows_of([local[0][0], local[1][0], local[0][1], local[1][1]], 128)
    pl.semaphore_wait(barrier, len(peers))

    g = share_z(net, stats)
    next(g)
    load_gain.wait()
    load_bias.wait()
    next(g)
    inverse = []
    for v in range(2):
        m = stats[:, v, :]
        mean = col_sum(m) / PLANES
        spread = col_sum(stats[:, 2 + v, :] + 128.0 * (m - mean) * (m - mean))
        inv = 1.0 / jnp.sqrt(spread / ROWS + eps_norm)
        inverse.append(inv)
        xh = (views[v].astype(F32) - mean) * inv
        pre = gain[...] * xh + bias[...]
        inner = 0.7978845608028654 * (pre + 0.044715 * (pre * pre * pre))
        th = jnp.tanh(inner)
        a = 0.5 * pre * (1.0 + th)
        act[y, x, core, v] = a.astype(BF16).reshape(2, 4, 16, 128)
        xhat[v] = xh
        slope[v] = 0.5 * (1.0 + th) + 0.5 * pre * (1.0 - th * th) * (
            0.7978845608028654 * (1.0 + 3.0 * 0.044715 * (pre * pre))
        )

    def z_terms(j):
        for h in range(2):
            if h == 0:
                f = mod4(x + (0, 3, 1, 2)[j])
                lhs = [act[k, f, q, 0].reshape(128, 128) for k in range(4) for q in range(2)]
                rhs = w[:, f].reshape(1024, 256)
            else:
                f = mod4(y + (0, 3, 1, 2)[j])
                lhs = [act[f, k, q, 1].reshape(128, 128) for k in range(4) for q in range(2)]
                rhs = w[f].reshape(1024, 256)
            term = dot_nn(jnp.concatenate(lhs, axis=1), rhs)
            if j == 0:
                zacc[h] = term
            else:
                zacc[h] = zacc[h] + term

    ag = gather_plane(net, act)
    next(ag)
    next(ag)
    next(ag)
    load.wait()
    for j in range(3):
        next(ag)
        next(ag)
        z_terms(j)
    next(ag)

    row_v, row_s, row_q = lax.div(chip, 8), lax.rem(lax.div(chip, 4), 2), lax.rem(chip, 4)

    def feature_rows(plane):
        owner = plane * 2 + core
        return act.at[lax.div(owner, 4), lax.rem(owner, 4), :, row_v, row_s, row_q]

    z_terms(3)
    zb = zacc[...].astype(BF16)
    zbuf[z] = zb.reshape(4, 64, 256)
    zf = zb.astype(F32)
    zsums = [col_sum(zf[v])[:, k : k + 128] for v in range(2) for k in (0, 128)]
    zsum[z] = jnp.concatenate(zsums, axis=0)
    means = share_z(net, zsum)
    next(means)
    own_rows = act_t.at[y, x, core, :, lax.div(z, 4), lax.rem(z, 4)]
    features = net.group(kgat.at[0, 0, 0:14])
    for d in (4, 3, 5, 2, 6, 1, 7):
        net.push(feature_rows(mod8(z + d)), own_rows, net.at_z(d), features)
    zring = ring_z(net, zbuf)
    next(zring)
    own_rows[...] = feature_rows(z)[...]
    colstat[...] = jnp.zeros_like(colstat)

    def block_in(stage, owner, v):
        slot = mod8(z + STAGES[stage][owner])
        zc = zbuf[slot, 2 * v : 2 * v + 2].reshape(128, 256).astype(F32) - zmean[v]
        cb = zc.astype(BF16)
        zcb[slot, v] = cb
        cf = cb.astype(F32)
        colstat[v : v + 1, :] += col_sum(zc * zc)
        colstat[2 + v : 3 + v, :] += col_sum(cf * cf)
        colstat[4 + v : 5 + v, :] += col_sum(cf)
        kpart[stage, owner, 8 * v : 8 * v + 8] = dot_nt(zcb[z, v], cb).reshape(8, 16, 128)

    k_over, k_in, k_gat, k_done = {}, {}, {}, {}
    k_sends = [
        net.sends(m) for m in (kpart.at[:, 0], kin, kgat.at[:, 0, 0:15], kgat.at[0:3, 0])
    ]

    def k_give(stage):
        k_over[stage] = net.push(
            kpart.at[stage, 1 - core], krecv.at[stage], net.partner(), sends=k_sends[0]
        )

    def k_spread(stage):
        k_over[stage].wait_recv()
        kmine[stage] = kpart[stage, core] + krecv[stage]
        group = net.group(kin.at[stage], k_sends[1])
        for k, (dy, dx) in enumerate(OFFSETS):
            ty, tx = mod4(y + dy), mod4(x + dx)
            net.push(kmine.at[stage, ty * SIDE + tx], kin.at[stage, k], net.at(ty, tx), group)
        k_in[stage] = group[2]

    def k_gather(stage):
        k_in[stage].wait_recv()
        total = kmine[stage, chip] + jnp.sum(kin[stage], axis=0)
        kown[stage] = total
        kgat[stage, core, chip] = total.astype(BF16)
        own = kgat.at[stage, core, chip]
        group = net.group(kgat.at[stage, core, 0:15], k_sends[2])
        both = net.group(kgat.at[stage, core]) if stage == 3 else None
        for dy, dx in OFFSETS:
            ty, tx = mod4(y + dy), mod4(x + dx)
            net.push(own, own, net.at(ty, tx), group)
            if both is not None:
                net.push(own, own, net.other(ty, tx), both)
        if both is not None:
            net.push(own, own, net.partner(), both)
            k_done[stage] = both[2]
        k_gat[stage] = group[2]

    def k_hand(stage):
        k_gat[stage].wait_recv()
        k_done[stage] = net.push(
            kgat.at[stage, core], kgat.at[stage, core], net.partner(), sends=k_sends[3]
        )

    def k_moved(stage):
        k_done[stage].wait_recv()
        slots = [mod8(z + r) for r in STAGES[stage]]
        for v in range(2):
            lhs = jnp.concatenate(
                [kgat[stage, q, 8 * v : 8 * v + 8].reshape(128, 128) for q in range(2)], axis=1
            )
            rhs = jnp.concatenate([zcb[slots[0], v], zcb[slots[1], v]], axis=0)
            term = dot_nn(lhs, rhs)
            if stage == 0:
                moved[v] = term
            else:
                moved[v] = moved[v] + term

    def step(count):
        for _ in range(count):
            next(zring)

    def blocks(stage):
        for v in range(2):
            block_in(stage, 0, v)
            block_in(stage, 1, v)

    step(6)
    next(means)
    ztotal = [
        jnp.concatenate([col_sum(zsum[:, 2 * v + k, :]) for k in range(2)], axis=1) for v in range(2)
    ]
    zmean = [t / ROWS for t in ztotal]
    block_in(3, 0, 0)
    block_in(3, 0, 1)
    blocks(0)
    k_give(0)
    features[2].wait_recv()
    agt = gather_plane(net, act_t, late=True)
    next(agt)
    step(2)
    blocks(1)
    k_give(1)
    k_spread(0)
    step(1)
    next(agt)
    step(2)
    k_spread(1)
    step(1)
    blocks(2)
    k_give(2)
    step(1)
    k_gather(0)
    k_spread(2)
    step(1)
    block_in(3, 1, 0)
    block_in(3, 1, 1)
    k_give(3)
    k_spread(3)

    for v in range(2):
        total = split3(colstat[4 + v : 5 + v, :])
        r = col_sum(dot_nt(total, zcb[:, v].reshape(1024, 256)))
        for slot in range(PLANES):
            rsum[v * PLANES + slot : v * PLANES + slot + 1, :] = r[:, 128 * slot : 128 * slot + 128]
    r_over = net.push(rsum, rcore, net.partner())
    k_gather(1)
    k_hand(0)
    k_gather(2)
    r_over.wait_recv()
    rmine[...] = rsum[...] + rcore[...]
    r_in = share_plane(net, rmine, rin)
    k_gather(3)
    k_hand(1)
    k_moved(0)
    k_hand(2)
    k_moved(1)
    r_in.wait_recv()
    row_total = rmine[...] + jnp.sum(rin[...], axis=0)
    std, diag, mean_t = [], [], []
    for v in range(2):
        std.append(jnp.sqrt(colstat[v : v + 1, :] / (ROWS - 1) + eps_std))
        diag.append(colstat[2 + v : 3 + v, :])
        row = jnp.concatenate(
            [row_total[v * PLANES + slot : v * PLANES + slot + 1, :] for slot in range(PLANES)], axis=1
        )
        m = col_sum(dot_nn(split3(row), zcb[:, v].reshape(1024, 256)))
        hinge = jnp.where(std[v] < 1.0, hinge_coef, 0.0) / std[v]
        mean_t.append(
            (
                coef * (m - diag[v] * colstat[4 + v : 5 + v, :])
                - hinge * (ztotal[v] - ROWS * zmean[v])
            )
            / ROWS
        )
    k_moved(2)
    k_gat[3].wait_recv()
    k_moved(3)
    zl = [zbuf[z, 2 * v : 2 * v + 2].reshape(128, 256).astype(F32) for v in range(2)]
    diff = zl[0] - zl[1]
    for v in range(2):
        hinge = jnp.where(std[v] < 1.0, hinge_coef, 0.0) / std[v]
        t = coef * (moved[v] - zcb[z, v].astype(F32) * diag[v]) - hinge * (zl[v] - zmean[v])
        sign = 1.0 if v == 0 else -1.0
        d = (t - mean_t[v] + (sign * inv_coef) * diff).astype(BF16)
        dz[z, 2 * v : 2 * v + 2] = d.reshape(2, 4, 16, 256)

    dring = ring_z(net, dz)
    next(dring)
    first_at, then_at = (x, y), (y, x)
    dzl = [dz[z, 2 * v : 2 * v + 2].reshape(128, 256) for v in range(2)]
    d_over, d_in, d_mid = {}, {}, {}
    d_sends = [net.sends(dgive), net.sends(dpart.at[:, 1:4]), net.sends(dmid_in)]

    def d_terms(h, g, parity, store):
        f = mod4(first_at[h] + g)
        rows = w[:, f, parity] if h == 0 else w[f, :, parity]
        t = dot_nt(dzl[h], rows.reshape(512, 256))
        for k in range(4):
            store[h, g, k] = t[:, 128 * k : 128 * k + 128]

    def d_ready(h, g):
        d_over[h, g].wait_recv()
        if g > 0:
            dpart[h, g] = (dkeep[h, g] + drecv[h, g]).astype(BF16)

    def d_send(h, g, pieces):
        to = net.along(h, mod4(first_at[h] + g), then_at[h])
        for k in pieces:
            t = mod4(then_at[h] + k)
            net.push(dpart.at[h, g, t], din.at[h, g - 1, t], to, d_in[h, k])

    for h in range(2):
        for k in range(4):
            d_in[h, k] = net.group(din.at[h, :, 0], d_sends[1])
    last = None
    for g in (2, 1, 3, 0):
        for h in range(2):
            d_terms(h, g, 1 - core, dgive)
            d_over[h, g] = net.push(
                dgive.at[h, g], drecv.at[h, g], net.partner(), sends=d_sends[0]
            )
        for h in range(2):
            d_terms(h, g, core, dkeep)
        if last is not None:
            for h in range(2):
                d_ready(h, last)
                d_send(h, last, (2, 1))
        last = g
    for g in (2, 1, 3):
        for h in range(2):
            d_send(h, g, (3, 0))
    next(dring)
    next(dring)
    for h in range(2):
        d_ready(h, 0)
    next(dring)

    def d_sum(h, k):
        t = mod4(then_at[h] + k)
        d_in[h, k][2].wait_recv()
        dmid[h, t] = (dkeep[h, 0, t] + drecv[h, 0, t]) + (
            din[h, 0, t].astype(F32) + din[h, 1, t].astype(F32) + din[h, 2, t].astype(F32)
        )
        if k > 0:
            net.push(
                dmid.at[h, t], dmid_in.at[h, k - 1], net.along(h, first_at[h], t), d_mid[h]
            )

    for h in range(2):
        d_mid[h] = net.group(dmid_in.at[h], d_sends[2])

    inv_row = col_sum(diff * diff)
    hinge_row = jnp.maximum(1.0 - std[0], 0.0) + jnp.maximum(1.0 - std[1], 0.0)
    diag_row = diag[0] * diag[0] + diag[1] * diag[1]
    wide = (25.0 / (ROWS * E)) * inv_row + (
        (25.0 / (2 * E)) * hinge_row - (1.0 / denom) * diag_row
    ) / PLANES
    ksq = col_sum(jnp.sum(kown[...] * kown[...], axis=0))
    share = wide[:, 0:128] + wide[:, 128:256] + (1.0 / denom) * ksq
    lsend[0] = rows_of([share], 128)
    loss_core = net.push(lsend.at[0], lrecv.at[15], net.partner())
    next(dring)
    for h in range(2):
        d_sum(h, 2)
    next(dring)
    for h in range(2):
        d_sum(h, 1)
    next(dring)
    loss_core.wait_recv()
    lsend[1] = lsend[0] + lrecv[15]
    loss_in = share_plane(net, lsend.at[1], lrecv.at[0:15])
    next(dring)
    for h in range(2):
        d_sum(h, 3)
    next(dring)
    for h in range(2):
        d_sum(h, 0)
    next(dring)
    next(dring)
    next(agt)
    loss_in.wait_recv()
    plane_loss = lsend[1, 0:1, :] + jnp.sum(lrecv[0:15, 0:1, :], axis=0)
    next(dring)
    next(dring)
    sums = []
    for h in range(2):
        d_mid[h][2].wait_recv()
        d_act = dmid[h, then_at[h]] + dmid_in[h, 0] + dmid_in[h, 1] + dmid_in[h, 2]
        dp = d_act * slope[h]
        dpre[h] = dp
        sums.append((col_sum(dp), col_sum(dp * xhat[h])))
    fstat[z] = rows_of([sums[0][0], sums[1][0], sums[0][1], sums[1][1], plane_loss], 128)
    final = share_z(net, fstat)
    next(final)
    next(dring)
    next(dring)
    next(agt)

    def gw_step(i, carry):
        lhs, rhs = [], []
        for k in range(2):
            c = 2 * i + k
            cy, cx = lax.div(c, 4), lax.rem(c, 4)
            lhs.append(
                jnp.concatenate(
                    [act_t[cy, cx, q // 2, q % 2].reshape(128, 128) for q in range(4)], axis=1
                )
            )
            rhs.append(dz[:, cy, cx].reshape(128, 256))
        term = dot_tn(jnp.concatenate(lhs, axis=0), jnp.concatenate(rhs, axis=0))
        grad_weight[...] = jnp.where(i == 0, term, grad_weight[...] + term)
        return carry

    grad_weight[...] = jnp.zeros_like(grad_weight)
    lax.fori_loop(0, 8, gw_step, 0)
    put = pltpu.make_async_copy(grad_weight, gw_hbm, load_sem.at[4])
    put.start()
    next(final)
    total_b = [col_sum(fstat[:, v, :]) for v in range(2)]
    total_g = [col_sum(fstat[:, 2 + v, :]) for v in range(2)]
    small[...] = rows_of([total_g[0] + total_g[1], total_b[0] + total_b[1], col_sum(fstat[:, 4, :])], 128)
    for v in range(2):
        views_gradient[v] = (gain[...] * inverse[v]) * (
            dpre[v] - total_b[v] / ROWS - xhat[v] * (total_g[v] / ROWS)
        )
    put.wait()
    for copy in net.open:
        copy.wait_send()


SENDS = 24
RECEIVES = 142


def finish(gw_in, small, vg_in, loss, grad_weight, grad_gain, grad_bias, views_gradient):
    grad_weight[...] = gw_in[...]
    views_gradient[...] = vg_in[...]
    grad_gain[...] = small[0:1, :]
    grad_bias[...] = small[1:2, :]
    loss[0, 0] = jnp.sum(small[2:3, :])


def shards(views, norm_scale_gain, norm_shift_bias, weight):
    vmem = pltpu.VMEM
    scratch = [
        vmem((2, 128, 128), BF16),
        vmem((1, 128), F32),
        vmem((1, 128), F32),
        vmem((512, 256), F32),
        vmem((4, 4, 2, 128, 256), BF16),
        vmem((4, 4, 2, 2, 2, 4, 16, 128), BF16),
        vmem((4, 4, 2, 2, 2, 4, 16, 128), BF16),
        vmem((2, 128, 128), F32),
        vmem((2, 128, 128), F32),
        vmem((8, 8, 128), F32),
        vmem((2, 128, 256), F32),
        vmem((8, 4, 64, 256), BF16),
        vmem((8, 4, 128), F32),
        vmem((8, 2, 128, 256), BF16),
        vmem((8, 256), F32),
        vmem((4, 2, 16, 16, 128), F32),
        vmem((4, 16, 16, 128), F32),
        vmem((4, 16, 16, 128), F32),
        vmem((4, 15, 16, 128), F32),
        vmem((4, 16, 128), F32),
        vmem((4, 2, 16, 16, 128), BF16),
        vmem((16, 128), F32),
        vmem((16, 128), F32),
        vmem((16, 128), F32),
        vmem((15, 16, 128), F32),
        vmem((2, 128, 256), F32),
        vmem((8, 4, 4, 16, 256), BF16),
        vmem((2, 4, 4, 128, 128), F32),
        vmem((2, 4, 4, 128, 128), F32),
        vmem((2, 4, 4, 128, 128), F32),
        vmem((2, 4, 4, 128, 128), BF16),
        vmem((2, 3, 4, 128, 128), BF16),
        vmem((2, 4, 128, 128), F32),
        vmem((2, 3, 128, 128), F32),
        vmem((2, 128, 128), F32),
        vmem((2, 8, 128), F32),
        vmem((16, 8, 128), F32),
        vmem((8, 8, 128), F32),
        pltpu.SemaphoreType.DMA((SENDS,)),
        pltpu.SemaphoreType.DMA((RECEIVES,)),
        pltpu.SemaphoreType.DMA((5,)),
    ]
    whole = pl.BlockSpec(memory_space=pltpu.VMEM)
    made = (
        jax.ShapeDtypeStruct((512, 256), F32),
        jax.ShapeDtypeStruct((8, 128), F32),
        jax.ShapeDtypeStruct((2, 128, 128), F32),
    )
    results = pl.pallas_call(
        body,
        out_shape=made,
        in_specs=[pl.BlockSpec(memory_space=pl.ANY)] * 4,
        out_specs=(pl.BlockSpec(memory_space=pl.ANY), whole, whole),
        scratch_shapes=scratch,
        compiler_params=pltpu.CompilerParams(collective_id=0, has_side_effects=True),
        name="vicreg_step",
    )(
        views,
        norm_scale_gain.reshape(1, 128),
        norm_shift_bias.reshape(1, 128),
        weight.reshape(4, 4, 2, 128, 256),
    )
    loss, grad_weight, grad_gain, grad_bias, views_gradient = pl.pallas_call(
        finish,
        out_shape=(
            jax.ShapeDtypeStruct((1, 1), F32),
            made[0],
            jax.ShapeDtypeStruct((1, 128), F32),
            jax.ShapeDtypeStruct((1, 128), F32),
            made[2],
        ),
        in_specs=[whole, whole, whole],
        out_specs=(pl.BlockSpec(memory_space=pltpu.SMEM), whole, whole, whole, whole),
        name="write_results",
    )(*results)
    return (
        loss.reshape(()),
        grad_weight,
        grad_gain.reshape(128),
        grad_bias.reshape(128),
        views_gradient,
    )


def solution(mesh):
    placed = (P(None, "batch", "col"), P("col"), P("col"), P(None, "col"))
    return jax.shard_map(
        shards,
        mesh=mesh,
        in_specs=placed,
        out_specs=(P(), P("batch", "col"), P("col"), P("col"), P(None, "batch", "col")),
        check_vma=False,
    )
```

```python
import jax
import jax.numpy as jnp
from jax import lax
from jax.experimental import pallas as pl
from jax.experimental.pallas import tpu as pltpu
from jax.sharding import PartitionSpec as P

E = 8192
ROWS = 1024
PLANES = 8
SIDE = 4

eps_norm = 1e-05
eps_std = 0.0001
scale = ROWS * E / 128.0
denom = float((ROWS - 1) ** 2 * E)
coef = 4.0 * scale / denom
hinge_coef = 25.0 * scale / (2.0 * E * (ROWS - 1))
inv_coef = 50.0 * scale / (ROWS * E)

F32 = jnp.float32
BF16 = jnp.bfloat16
MESH = pl.DeviceIdType.MESH


def dot_nt(a, b):
    return lax.dot_general(a, b, (((1,), (1,)), ((), ())), preferred_element_type=F32)


def dot_tn(a, b):
    return lax.dot_general(a, b, (((0,), (0,)), ((), ())), preferred_element_type=F32)


def dot_nn(a, b):
    return jnp.dot(a, b, preferred_element_type=F32)


class Net:
    def __init__(self, send, recv):
        self.send, self.recv, self.n_send, self.n_recv, self.open = send, recv, 0, 0, []
        self.z = lax.axis_index("batch")
        self.c = lax.axis_index("col")
        self.core = lax.rem(self.c, 2)
        self.chip = lax.div(self.c, 2)
        self.x = lax.rem(self.chip, SIDE)
        self.y = lax.div(self.chip, SIDE)

    def at_z(self, d):
        return (mod8(self.z + d), self.c)

    def at(self, y, x):
        return (self.z, (y * SIDE + x) * 2 + self.core)

    def other(self, y, x):
        return (self.z, (y * SIDE + x) * 2 + 1 - self.core)

    def along(self, h, f, t):
        return self.at(t, f) if h == 0 else self.at(f, t)

    def partner(self):
        return (self.z, self.chip * 2 + 1 - self.core)

    def copy(self, src, dst, device, send, recv):
        return pltpu.make_async_remote_copy(
            src_ref=src,
            dst_ref=dst,
            send_sem=self.send.at[send],
            recv_sem=self.recv.at[recv],
            device_id=device,
            device_id_type=MESH,
        )

    def sends(self, meter):
        i = self.n_send
        self.n_send += 1
        self.open.append(self.copy(meter, meter, self.partner(), i, 0))
        return i

    def group(self, meter, sends=None):
        send = self.sends(meter) if sends is None else sends
        i = self.n_recv
        self.n_recv += 1
        return send, i, self.copy(meter, meter, self.partner(), send, i)

    def push(self, src, dst, device, group=None, sends=None):
        if group is not None:
            self.copy(src, dst, device, group[0], group[1]).start()
            return None
        send = self.sends(src) if sends is None else sends
        i = self.n_recv
        self.n_recv += 1
        one = self.copy(src, dst, device, send, i)
        one.start()
        return one

    def peers(self):
        found = [self.partner()]
        found += [self.at_z(d) for d in range(1, PLANES)]
        for dy, dx in OFFSETS:
            found.append(self.at(mod4(self.y + dy), mod4(self.x + dx)))
            found.append(self.other(mod4(self.y + dy), mod4(self.x + dx)))
        return found


OFFSETS = [(dy, dx) for dy in (2, 1, 3, 0) for dx in (2, 1, 3, 0) if (dy, dx) != (0, 0)]


def mod4(a):
    return lax.rem(a, SIDE)


def mod8(a):
    return lax.rem(a, PLANES)


def share_z(net, buf):
    group = net.group(buf.at[0:7])
    for d in (4, 3, 5, 2, 6, 1, 7):
        net.push(buf.at[net.z], buf.at[net.z], net.at_z(d), group)
    yield
    group[2].wait_recv()
    yield


def share_plane(net, src, dst):
    group = net.group(dst)
    for k, (dy, dx) in enumerate(OFFSETS):
        net.push(src, dst.at[k], net.at(mod4(net.y + dy), mod4(net.x + dx)), group)
    return group[2]


def ring_z(net, buf):
    sends = net.sends(buf.at[0:7])
    up, down = {}, {}
    for q in range(4):
        own = buf.at[net.z, q]
        up[1, q] = net.push(own, own, net.at_z(1), sends=sends)
        down[1, q] = net.push(own, own, net.at_z(7), sends=sends)
    yield
    for d in range(1, 5):
        for q in range(4 if d < 4 else 2):
            up[d, q].wait_recv()
            if d < 3 or (d == 3 and q < 2):
                block = buf.at[mod8(net.z + 8 - d), q]
                up[d + 1, q] = net.push(block, block, net.at_z(1), sends=sends)
            q = q if d < 4 else q + 2
            down[d, q].wait_recv()
            if d < 3 or (d == 3 and q >= 2):
                block = buf.at[mod8(net.z + d), q]
                down[d + 1, q] = net.push(block, block, net.at_z(7), sends=sends)
            yield


def gather_plane(net, buf, late=False):
    first_at, then_at = (net.x, net.y), (net.y, net.x)
    shift = (0, 3, 1, 2)
    first, cross, over = {}, {}, {}
    first_sends = net.sends(buf.at[0:3, 0, 0])
    cross_sends = net.sends(buf.at[0:3, :, 0])
    over_sends = net.sends(buf.at[:, :, 0])

    def piece(h, f, t):
        y, x = (t, f) if h == 0 else (f, t)
        return buf.at[y, x, net.core, h]

    def spread(h, j):
        f = mod4(first_at[h] + shift[j])
        cross[h, j] = net.group(buf.at[0:3, 0, 0, 0], cross_sends)
        block = piece(h, f, then_at[h])
        for d in (2, 1, 3):
            net.push(block, block, net.along(h, f_own[h], mod4(then_at[h] + d)), cross[h, j])

    def hand_over(h, j):
        cross[h, j][2].wait_recv()
        f = mod4(first_at[h] + shift[j])
        line = buf.at[:, f, net.core, 0] if h == 0 else buf.at[f, :, net.core, 1]
        over[h, j] = net.push(line, line, net.partner(), sends=over_sends)

    f_own = first_at
    for h in range(2):
        block = piece(h, first_at[h], then_at[h])
        for d in (1, 3, 2):
            to = net.along(h, mod4(first_at[h] + d), then_at[h])
            first[h, d] = net.push(block, block, to, sends=first_sends)
    if late:
        yield
    for h in range(2):
        spread(h, 0)
    if not late:
        yield
    for j, d in ((1, 1), (2, 3), (3, 2)):
        for h in range(2):
            first[h, d].wait_recv()
            spread(h, j)
    yield
    if late:
        for j in range(4):
            for h in range(2):
                hand_over(h, j)
        yield
        for copy in over.values():
            copy.wait_recv()
        yield
        return
    for j in range(4):
        for h in range(2):
            hand_over(h, j)
        yield
        if j > 0:
            for h in range(2):
                over[h, j - 1].wait_recv()
            yield
    for h in range(2):
        over[h, 3].wait_recv()
    yield


def rows_of(parts, width):
    count = len(parts)
    rows = list(parts)
    if count < 8:
        rows.append(jnp.zeros((8 - count, width), F32))
    return jnp.concatenate(rows, axis=0)


def col_sum(t):
    return jnp.sum(t, axis=0, keepdims=True)


def split3(t):
    hi = t.astype(BF16)
    rest = t - hi.astype(F32)
    mid = rest.astype(BF16)
    lo = (rest - mid.astype(F32)).astype(BF16)
    zero = jnp.zeros((5, t.shape[1]), F32)
    return jnp.concatenate([hi.astype(F32), mid.astype(F32), lo.astype(F32), zero], axis=0).astype(BF16)


STAGES = ((1, 7), (2, 6), (3, 5), (0, 4))


def body(
    views_hbm,
    gain_hbm,
    bias_hbm,
    w_hbm,
    gw_hbm,
    small,
    views_gradient,
    views,
    gain,
    bias,
    grad_weight,
    w,
    act,
    act_t,
    xhat,
    slope,
    stats,
    zacc,
    zbuf,
    zsum,
    zcb,
    colstat,
    kpart,
    krecv,
    kmine,
    kin,
    kown,
    kgat,
    rsum,
    rcore,
    rmine,
    rin,
    moved,
    dz,
    dgive,
    dkeep,
    drecv,
    dpart,
    din,
    dmid,
    dmid_in,
    dpre,
    lsend,
    lrecv,
    fstat,
    send_sems,
    recv_sems,
    load_sem,
):
    net = Net(send_sems, recv_sems)
    z, y, x, core, chip = net.z, net.y, net.x, net.core, net.chip
    load_views = pltpu.make_async_copy(views_hbm, views, load_sem.at[0])
    load_gain = pltpu.make_async_copy(gain_hbm, gain, load_sem.at[1])
    load_bias = pltpu.make_async_copy(bias_hbm, bias, load_sem.at[2])
    load = pltpu.make_async_copy(w_hbm, w, load_sem.at[3])
    load_views.start()
    barrier = pltpu.get_barrier_semaphore()
    peers = net.peers()
    for peer in peers:
        pl.semaphore_signal(barrier, inc=1, device_id=peer, device_id_type=MESH)
    load_gain.start()
    load_bias.start()
    load.start()
    load_views.wait()
    local = []
    for v in range(2):
        t = views[v].astype(F32)
        m = col_sum(t) / 128.0
        local.append((m, col_sum((t - m) * (t - m))))
    stats[z] = rows_of([local[0][0], local[1][0], local[0][1], local[1][1]], 128)
    pl.semaphore_wait(barrier, len(peers))

    g = share_z(net, stats)
    next(g)
    load_gain.wait()
    load_bias.wait()
    next(g)
    inverse = []
    for v in range(2):
        m = stats[:, v, :]
        mean = col_sum(m) / PLANES
        spread = col_sum(stats[:, 2 + v, :] + 128.0 * (m - mean) * (m - mean))
        inv = 1.0 / jnp.sqrt(spread / ROWS + eps_norm)
        inverse.append(inv)
        xh = (views[v].astype(F32) - mean) * inv
        pre = gain[...] * xh + bias[...]
        inner = 0.7978845608028654 * (pre + 0.044715 * (pre * pre * pre))
        th = jnp.tanh(inner)
        a = 0.5 * pre * (1.0 + th)
        act[y, x, core, v] = a.astype(BF16).reshape(2, 4, 16, 128)
        xhat[v] = xh
        slope[v] = 0.5 * (1.0 + th) + 0.5 * pre * (1.0 - th * th) * (
            0.7978845608028654 * (1.0 + 3.0 * 0.044715 * (pre * pre))
        )

    def z_terms(j):
        for h in range(2):
            if h == 0:
                f = mod4(x + (0, 3, 1, 2)[j])
                lhs = [act[k, f, q, 0].reshape(128, 128) for k in range(4) for q in range(2)]
                rhs = w[:, f].reshape(1024, 256)
            else:
                f = mod4(y + (0, 3, 1, 2)[j])
                lhs = [act[f, k, q, 1].reshape(128, 128) for k in range(4) for q in range(2)]
                rhs = w[f].reshape(1024, 256)
            term = dot_nn(jnp.concatenate(lhs, axis=1), rhs)
            if j == 0:
                zacc[h] = term
            else:
                zacc[h] = zacc[h] + term

    ag = gather_plane(net, act)
    next(ag)
    next(ag)
    next(ag)
    load.wait()
    for j in range(3):
        next(ag)
        next(ag)
        z_terms(j)
    next(ag)

    row_v, row_s, row_q = lax.div(chip, 8), lax.rem(lax.div(chip, 4), 2), lax.rem(chip, 4)

    def feature_rows(plane):
        owner = plane * 2 + core
        return act.at[lax.div(owner, 4), lax.rem(owner, 4), :, row_v, row_s, row_q]

    z_terms(3)
    zb = zacc[...].astype(BF16)
    zbuf[z] = zb.reshape(4, 64, 256)
    zf = zb.astype(F32)
    zsums = [col_sum(zf[v])[:, k : k + 128] for v in range(2) for k in (0, 128)]
    zsum[z] = jnp.concatenate(zsums, axis=0)
    means = share_z(net, zsum)
    next(means)
    own_rows = act_t.at[y, x, core, :, lax.div(z, 4), lax.rem(z, 4)]
    zring = ring_z(net, zbuf)
    next(zring)
    features = net.group(kgat.at[0, 0, 0:14])
    for d in (4, 3, 5, 2, 6, 1, 7):
        net.push(feature_rows(mod8(z + d)), own_rows, net.at_z(d), features)
    own_rows[...] = feature_rows(z)[...]
    colstat[...] = jnp.zeros_like(colstat)

    def block_in(stage, owner, v):
        slot = mod8(z + STAGES[stage][owner])
        zc = zbuf[slot, 2 * v : 2 * v + 2].reshape(128, 256).astype(F32) - zmean[v]
        cb = zc.astype(BF16)
        zcb[slot, v] = cb
        cf = cb.astype(F32)
        colstat[v : v + 1, :] += col_sum(zc * zc)
        colstat[2 + v : 3 + v, :] += col_sum(cf * cf)
        colstat[4 + v : 5 + v, :] += col_sum(cf)
        kpart[stage, owner, 8 * v : 8 * v + 8] = dot_nt(zcb[z, v], cb).reshape(8, 16, 128)

    k_over, k_in, k_gat, k_done = {}, {}, {}, {}
    k_sends = [
        net.sends(m) for m in (kpart.at[:, 0], kin, kgat.at[:, 0, 0:15], kgat.at[0:3, 0])
    ]

    def k_give(stage):
        k_over[stage] = net.push(
            kpart.at[stage, 1 - core], krecv.at[stage], net.partner(), sends=k_sends[0]
        )

    def k_spread(stage):
        k_over[stage].wait_recv()
        kmine[stage] = kpart[stage, core] + krecv[stage]
        group = net.group(kin.at[stage], k_sends[1])
        for k, (dy, dx) in enumerate(OFFSETS):
            ty, tx = mod4(y + dy), mod4(x + dx)
            net.push(kmine.at[stage, ty * SIDE + tx], kin.at[stage, k], net.at(ty, tx), group)
        k_in[stage] = group[2]

    def k_gather(stage):
        k_in[stage].wait_recv()
        total = kmine[stage, chip] + jnp.sum(kin[stage], axis=0)
        kown[stage] = total
        kgat[stage, core, chip] = total.astype(BF16)
        own = kgat.at[stage, core, chip]
        group = net.group(kgat.at[stage, core, 0:15], k_sends[2])
        both = net.group(kgat.at[stage, core]) if stage == 3 else None
        for dy, dx in OFFSETS:
            ty, tx = mod4(y + dy), mod4(x + dx)
            net.push(own, own, net.at(ty, tx), group)
            if both is not None:
                net.push(own, own, net.other(ty, tx), both)
        if both is not None:
            net.push(own, own, net.partner(), both)
            k_done[stage] = both[2]
        k_gat[stage] = group[2]

    def k_hand(stage):
        k_gat[stage].wait_recv()
        k_done[stage] = net.push(
            kgat.at[stage, core], kgat.at[stage, core], net.partner(), sends=k_sends[3]
        )

    def k_moved(stage):
        k_done[stage].wait_recv()
        slots = [mod8(z + r) for r in STAGES[stage]]
        for v in range(2):
            lhs = jnp.concatenate(
                [kgat[stage, q, 8 * v : 8 * v + 8].reshape(128, 128) for q in range(2)], axis=1
            )
            rhs = jnp.concatenate([zcb[slots[0], v], zcb[slots[1], v]], axis=0)
            term = dot_nn(lhs, rhs)
            if stage == 0:
                moved[v] = term
            else:
                moved[v] = moved[v] + term

    def step(count):
        for _ in range(count):
            next(zring)

    def blocks(stage):
        for v in range(2):
            block_in(stage, 0, v)
            block_in(stage, 1, v)

    step(6)
    next(means)
    ztotal = [
        jnp.concatenate([col_sum(zsum[:, 2 * v + k, :]) for k in range(2)], axis=1) for v in range(2)
    ]
    zmean = [t / ROWS for t in ztotal]
    block_in(3, 0, 0)
    block_in(3, 0, 1)
    blocks(0)
    k_give(0)
    step(2)
    blocks(1)
    k_give(1)
    k_spread(0)
    step(1)
    features[2].wait_recv()
    agt = gather_plane(net, act_t, late=True)
    next(agt)
    step(2)
    k_spread(1)
    step(1)
    blocks(2)
    k_give(2)
    step(1)
    k_gather(0)
    k_spread(2)
    step(1)
    block_in(3, 1, 0)
    block_in(3, 1, 1)
    k_give(3)
    k_spread(3)

    for v in range(2):
        total = split3(colstat[4 + v : 5 + v, :])
        r = col_sum(dot_nt(total, zcb[:, v].reshape(1024, 256)))
        for slot in range(PLANES):
            rsum[v * PLANES + slot : v * PLANES + slot + 1, :] = r[:, 128 * slot : 128 * slot + 128]
    r_over = net.push(rsum, rcore, net.partner())
    k_gather(1)
    k_hand(0)
    k_gather(2)
    r_over.wait_recv()
    rmine[...] = rsum[...] + rcore[...]
    r_in = share_plane(net, rmine, rin)
    k_gather(3)
    next(agt)
    k_hand(1)
    k_moved(0)
    k_hand(2)
    k_moved(1)
    r_in.wait_recv()
    row_total = rmine[...] + jnp.sum(rin[...], axis=0)
    std, diag, mean_t = [], [], []
    for v in range(2):
        std.append(jnp.sqrt(colstat[v : v + 1, :] / (ROWS - 1) + eps_std))
        diag.append(colstat[2 + v : 3 + v, :])
        row = jnp.concatenate(
            [row_total[v * PLANES + slot : v * PLANES + slot + 1, :] for slot in range(PLANES)], axis=1
        )
        m = col_sum(dot_nn(split3(row), zcb[:, v].reshape(1024, 256)))
        hinge = jnp.where(std[v] < 1.0, hinge_coef, 0.0) / std[v]
        mean_t.append(
            (
                coef * (m - diag[v] * colstat[4 + v : 5 + v, :])
                - hinge * (ztotal[v] - ROWS * zmean[v])
            )
            / ROWS
        )
    k_moved(2)
    k_gat[3].wait_recv()
    k_moved(3)
    zl = [zbuf[z, 2 * v : 2 * v + 2].reshape(128, 256).astype(F32) for v in range(2)]
    diff = zl[0] - zl[1]
    for v in range(2):
        hinge = jnp.where(std[v] < 1.0, hinge_coef, 0.0) / std[v]
        t = coef * (moved[v] - zcb[z, v].astype(F32) * diag[v]) - hinge * (zl[v] - zmean[v])
        sign = 1.0 if v == 0 else -1.0
        d = (t - mean_t[v] + (sign * inv_coef) * diff).astype(BF16)
        dz[z, 2 * v : 2 * v + 2] = d.reshape(2, 4, 16, 256)

    dring = ring_z(net, dz)
    next(dring)
    first_at, then_at = (x, y), (y, x)
    dzl = [dz[z, 2 * v : 2 * v + 2].reshape(128, 256) for v in range(2)]
    d_over, d_in, d_mid = {}, {}, {}
    d_sends = [net.sends(dgive), net.sends(dpart.at[:, 1:4]), net.sends(dmid_in)]

    def d_terms(h, g, parity, store):
        f = mod4(first_at[h] + g)
        rows = w[:, f, parity] if h == 0 else w[f, :, parity]
        t = dot_nt(dzl[h], rows.reshape(512, 256))
        for k in range(4):
            store[h, g, k] = t[:, 128 * k : 128 * k + 128]

    def d_ready(h, g):
        d_over[h, g].wait_recv()
        if g > 0:
            dpart[h, g] = (dkeep[h, g] + drecv[h, g]).astype(BF16)

    def d_send(h, g, pieces):
        to = net.along(h, mod4(first_at[h] + g), then_at[h])
        for k in pieces:
            t = mod4(then_at[h] + k)
            net.push(dpart.at[h, g, t], din.at[h, g - 1, t], to, d_in[h, k])

    for h in range(2):
        for k in range(4):
            d_in[h, k] = net.group(din.at[h, :, 0], d_sends[1])
    last = None
    for g in (2, 1, 3, 0):
        for h in range(2):
            d_terms(h, g, 1 - core, dgive)
            d_over[h, g] = net.push(
                dgive.at[h, g], drecv.at[h, g], net.partner(), sends=d_sends[0]
            )
        for h in range(2):
            d_terms(h, g, core, dkeep)
        if last is not None:
            for h in range(2):
                d_ready(h, last)
                d_send(h, last, (2, 1))
        last = g
    for g in (2, 1, 3):
        for h in range(2):
            d_send(h, g, (3, 0))
    next(dring)
    next(dring)
    for h in range(2):
        d_ready(h, 0)
    next(dring)

    def d_sum(h, k):
        t = mod4(then_at[h] + k)
        d_in[h, k][2].wait_recv()
        dmid[h, t] = (dkeep[h, 0, t] + drecv[h, 0, t]) + (
            din[h, 0, t].astype(F32) + din[h, 1, t].astype(F32) + din[h, 2, t].astype(F32)
        )
        if k > 0:
            net.push(
                dmid.at[h, t], dmid_in.at[h, k - 1], net.along(h, first_at[h], t), d_mid[h]
            )

    for h in range(2):
        d_mid[h] = net.group(dmid_in.at[h], d_sends[2])

    inv_row = col_sum(diff * diff)
    hinge_row = jnp.maximum(1.0 - std[0], 0.0) + jnp.maximum(1.0 - std[1], 0.0)
    diag_row = diag[0] * diag[0] + diag[1] * diag[1]
    wide = (25.0 / (ROWS * E)) * inv_row + (
        (25.0 / (2 * E)) * hinge_row - (1.0 / denom) * diag_row
    ) / PLANES
    ksq = col_sum(jnp.sum(kown[...] * kown[...], axis=0))
    share = wide[:, 0:128] + wide[:, 128:256] + (1.0 / denom) * ksq
    lsend[0] = rows_of([share], 128)
    loss_core = net.push(lsend.at[0], lrecv.at[15], net.partner())
    next(dring)
    for h in range(2):
        d_sum(h, 2)
    next(dring)
    for h in range(2):
        d_sum(h, 1)
    next(dring)
    loss_core.wait_recv()
    lsend[1] = lsend[0] + lrecv[15]
    loss_in = share_plane(net, lsend.at[1], lrecv.at[0:15])
    next(dring)
    for h in range(2):
        d_sum(h, 3)
    next(dring)
    for h in range(2):
        d_sum(h, 0)
    next(dring)
    next(dring)
    next(agt)
    loss_in.wait_recv()
    plane_loss = lsend[1, 0:1, :] + jnp.sum(lrecv[0:15, 0:1, :], axis=0)
    next(dring)
    next(dring)
    sums = []
    for h in range(2):
        d_mid[h][2].wait_recv()
        d_act = dmid[h, then_at[h]] + dmid_in[h, 0] + dmid_in[h, 1] + dmid_in[h, 2]
        dp = d_act * slope[h]
        dpre[h] = dp
        sums.append((col_sum(dp), col_sum(dp * xhat[h])))
    fstat[z] = rows_of([sums[0][0], sums[1][0], sums[0][1], sums[1][1], plane_loss], 128)
    final = share_z(net, fstat)
    next(final)
    next(dring)
    next(dring)
    next(agt)

    def gw_step(i, carry):
        lhs, rhs = [], []
        for k in range(2):
            c = 2 * i + k
            cy, cx = lax.div(c, 4), lax.rem(c, 4)
            lhs.append(
                jnp.concatenate(
                    [act_t[cy, cx, q // 2, q % 2].reshape(128, 128) for q in range(4)], axis=1
                )
            )
            rhs.append(dz[:, cy, cx].reshape(128, 256))
        term = dot_tn(jnp.concatenate(lhs, axis=0), jnp.concatenate(rhs, axis=0))
        grad_weight[...] = jnp.where(i == 0, term, grad_weight[...] + term)
        return carry

    grad_weight[...] = jnp.zeros_like(grad_weight)
    lax.fori_loop(0, 8, gw_step, 0)
    put = pltpu.make_async_copy(grad_weight, gw_hbm, load_sem.at[4])
    put.start()
    next(final)
    total_b = [col_sum(fstat[:, v, :]) for v in range(2)]
    total_g = [col_sum(fstat[:, 2 + v, :]) for v in range(2)]
    small[...] = rows_of([total_g[0] + total_g[1], total_b[0] + total_b[1], col_sum(fstat[:, 4, :])], 128)
    for v in range(2):
        views_gradient[v] = (gain[...] * inverse[v]) * (
            dpre[v] - total_b[v] / ROWS - xhat[v] * (total_g[v] / ROWS)
        )
    put.wait()
    for copy in net.open:
        copy.wait_send()


SENDS = 24
RECEIVES = 142


def finish(gw_in, small, vg_in, loss, grad_weight, grad_gain, grad_bias, views_gradient):
    grad_weight[...] = gw_in[...]
    views_gradient[...] = vg_in[...]
    grad_gain[...] = small[0:1, :]
    grad_bias[...] = small[1:2, :]
    loss[0, 0] = jnp.sum(small[2:3, :])


def shards(views, norm_scale_gain, norm_shift_bias, weight):
    vmem = pltpu.VMEM
    scratch = [
        vmem((2, 128, 128), BF16),
        vmem((1, 128), F32),
        vmem((1, 128), F32),
        vmem((512, 256), F32),
        vmem((4, 4, 2, 128, 256), BF16),
        vmem((4, 4, 2, 2, 2, 4, 16, 128), BF16),
        vmem((4, 4, 2, 2, 2, 4, 16, 128), BF16),
        vmem((2, 128, 128), F32),
        vmem((2, 128, 128), F32),
        vmem((8, 8, 128), F32),
        vmem((2, 128, 256), F32),
        vmem((8, 4, 64, 256), BF16),
        vmem((8, 4, 128), F32),
        vmem((8, 2, 128, 256), BF16),
        vmem((8, 256), F32),
        vmem((4, 2, 16, 16, 128), F32),
        vmem((4, 16, 16, 128), F32),
        vmem((4, 16, 16, 128), F32),
        vmem((4, 15, 16, 128), F32),
        vmem((4, 16, 128), F32),
        vmem((4, 2, 16, 16, 128), BF16),
        vmem((16, 128), F32),
        vmem((16, 128), F32),
        vmem((16, 128), F32),
        vmem((15, 16, 128), F32),
        vmem((2, 128, 256), F32),
        vmem((8, 4, 4, 16, 256), BF16),
        vmem((2, 4, 4, 128, 128), F32),
        vmem((2, 4, 4, 128, 128), F32),
        vmem((2, 4, 4, 128, 128), F32),
        vmem((2, 4, 4, 128, 128), BF16),
        vmem((2, 3, 4, 128, 128), BF16),
        vmem((2, 4, 128, 128), F32),
        vmem((2, 3, 128, 128), F32),
        vmem((2, 128, 128), F32),
        vmem((2, 8, 128), F32),
        vmem((16, 8, 128), F32),
        vmem((8, 8, 128), F32),
        pltpu.SemaphoreType.DMA((SENDS,)),
        pltpu.SemaphoreType.DMA((RECEIVES,)),
        pltpu.SemaphoreType.DMA((5,)),
    ]
    whole = pl.BlockSpec(memory_space=pltpu.VMEM)
    made = (
        jax.ShapeDtypeStruct((512, 256), F32),
        jax.ShapeDtypeStruct((8, 128), F32),
        jax.ShapeDtypeStruct((2, 128, 128), F32),
    )
    results = pl.pallas_call(
        body,
        out_shape=made,
        in_specs=[pl.BlockSpec(memory_space=pl.ANY)] * 4,
        out_specs=(pl.BlockSpec(memory_space=pl.ANY), whole, whole),
        scratch_shapes=scratch,
        compiler_params=pltpu.CompilerParams(collective_id=0, has_side_effects=True),
        name="vicreg_step",
    )(
        views,
        norm_scale_gain.reshape(1, 128),
        norm_shift_bias.reshape(1, 128),
        weight.reshape(4, 4, 2, 128, 256),
    )
    loss, grad_weight, grad_gain, grad_bias, views_gradient = pl.pallas_call(
        finish,
        out_shape=(
            jax.ShapeDtypeStruct((1, 1), F32),
            made[0],
            jax.ShapeDtypeStruct((1, 128), F32),
            jax.ShapeDtypeStruct((1, 128), F32),
            made[2],
        ),
        in_specs=[whole, whole, whole],
        out_specs=(pl.BlockSpec(memory_space=pltpu.SMEM), whole, whole, whole, whole),
        name="write_results",
    )(*results)
    return (
        loss.reshape(()),
        grad_weight,
        grad_gain.reshape(128),
        grad_bias.reshape(128),
        views_gradient,
    )


def solution(mesh):
    placed = (P(None, "batch", "col"), P("col"), P("col"), P(None, "col"))
    return jax.shard_map(
        shards,
        mesh=mesh,
        in_specs=placed,
        out_specs=(P(), P("batch", "col"), P("col"), P("col"), P(None, "batch", "col")),
        check_vma=False,
    )
```

```python
import jax
import jax.numpy as jnp
from jax import lax
from jax.experimental import pallas as pl
from jax.experimental.pallas import tpu as pltpu
from jax.sharding import PartitionSpec as P

E = 8192
ROWS = 1024
PLANES = 8
SIDE = 4

eps_norm = 1e-05
eps_std = 0.0001
scale = ROWS * E / 128.0
denom = float((ROWS - 1) ** 2 * E)
coef = 4.0 * scale / denom
hinge_coef = 25.0 * scale / (2.0 * E * (ROWS - 1))
inv_coef = 50.0 * scale / (ROWS * E)

F32 = jnp.float32
BF16 = jnp.bfloat16
MESH = pl.DeviceIdType.MESH


def dot_nt(a, b):
    return lax.dot_general(a, b, (((1,), (1,)), ((), ())), preferred_element_type=F32)


def dot_tn(a, b):
    return lax.dot_general(a, b, (((0,), (0,)), ((), ())), preferred_element_type=F32)


def dot_nn(a, b):
    return jnp.dot(a, b, preferred_element_type=F32)


class Net:
    def __init__(self, send, recv):
        self.send, self.recv, self.n_send, self.n_recv, self.open = send, recv, 0, 0, []
        self.z = lax.axis_index("batch")
        self.c = lax.axis_index("col")
        self.core = lax.rem(self.c, 2)
        self.chip = lax.div(self.c, 2)
        self.x = lax.rem(self.chip, SIDE)
        self.y = lax.div(self.chip, SIDE)

    def at_z(self, d):
        return (mod8(self.z + d), self.c)

    def at(self, y, x):
        return (self.z, (y * SIDE + x) * 2 + self.core)

    def other(self, y, x):
        return (self.z, (y * SIDE + x) * 2 + 1 - self.core)

    def along(self, h, f, t):
        return self.at(t, f) if h == 0 else self.at(f, t)

    def partner(self):
        return (self.z, self.chip * 2 + 1 - self.core)

    def copy(self, src, dst, device, send, recv):
        return pltpu.make_async_remote_copy(
            src_ref=src,
            dst_ref=dst,
            send_sem=self.send.at[send],
            recv_sem=self.recv.at[recv],
            device_id=device,
            device_id_type=MESH,
        )

    def sends(self, meter):
        i = self.n_send
        self.n_send += 1
        self.open.append(self.copy(meter, meter, self.partner(), i, 0))
        return i

    def group(self, meter, sends=None):
        send = self.sends(meter) if sends is None else sends
        i = self.n_recv
        self.n_recv += 1
        return send, i, self.copy(meter, meter, self.partner(), send, i)

    def push(self, src, dst, device, group=None, sends=None):
        if group is not None:
            self.copy(src, dst, device, group[0], group[1]).start()
            return None
        send = self.sends(src) if sends is None else sends
        i = self.n_recv
        self.n_recv += 1
        one = self.copy(src, dst, device, send, i)
        one.start()
        return one

    def peers(self):
        found = [self.partner()]
        found += [self.at_z(d) for d in range(1, PLANES)]
        for dy, dx in OFFSETS:
            found.append(self.at(mod4(self.y + dy), mod4(self.x + dx)))
            found.append(self.other(mod4(self.y + dy), mod4(self.x + dx)))
        return found


OFFSETS = [(dy, dx) for dy in (2, 1, 3, 0) for dx in (2, 1, 3, 0) if (dy, dx) != (0, 0)]


def mod4(a):
    return lax.rem(a, SIDE)


def mod8(a):
    return lax.rem(a, PLANES)


def share_z(net, buf):
    group = net.group(buf.at[0:7])
    for d in (4, 3, 5, 2, 6, 1, 7):
        net.push(buf.at[net.z], buf.at[net.z], net.at_z(d), group)
    yield
    group[2].wait_recv()
    yield


def share_plane(net, src, dst):
    group = net.group(dst)
    for k, (dy, dx) in enumerate(OFFSETS):
        net.push(src, dst.at[k], net.at(mod4(net.y + dy), mod4(net.x + dx)), group)
    return group[2]


def ring_z(net, buf):
    sends = net.sends(buf.at[0:7])
    up, down = {}, {}
    for q in range(4):
        own = buf.at[net.z, q]
        up[1, q] = net.push(own, own, net.at_z(1), sends=sends)
        down[1, q] = net.push(own, own, net.at_z(7), sends=sends)
    yield
    for d in range(1, 5):
        for q in range(4 if d < 4 else 2):
            up[d, q].wait_recv()
            if d < 3 or (d == 3 and q < 2):
                block = buf.at[mod8(net.z + 8 - d), q]
                up[d + 1, q] = net.push(block, block, net.at_z(1), sends=sends)
            q = q if d < 4 else q + 2
            down[d, q].wait_recv()
            if d < 3 or (d == 3 and q >= 2):
                block = buf.at[mod8(net.z + d), q]
                down[d + 1, q] = net.push(block, block, net.at_z(7), sends=sends)
            yield


def gather_plane(net, buf, late=False):
    first_at, then_at = (net.x, net.y), (net.y, net.x)
    shift = (0, 3, 1, 2)
    first, cross, over = {}, {}, {}
    first_sends = net.sends(buf.at[0:3, 0, 0])
    cross_sends = net.sends(buf.at[0:3, :, 0])
    over_sends = net.sends(buf.at[:, :, 0])

    def piece(h, f, t):
        y, x = (t, f) if h == 0 else (f, t)
        return buf.at[y, x, net.core, h]

    def spread(h, j):
        f = mod4(first_at[h] + shift[j])
        cross[h, j] = net.group(buf.at[0:3, 0, 0, 0], cross_sends)
        block = piece(h, f, then_at[h])
        for d in (2, 1, 3):
            net.push(block, block, net.along(h, f_own[h], mod4(then_at[h] + d)), cross[h, j])

    def hand_over(h, j):
        cross[h, j][2].wait_recv()
        f = mod4(first_at[h] + shift[j])
        line = buf.at[:, f, net.core, 0] if h == 0 else buf.at[f, :, net.core, 1]
        over[h, j] = net.push(line, line, net.partner(), sends=over_sends)

    f_own = first_at
    for h in range(2):
        block = piece(h, first_at[h], then_at[h])
        for d in (1, 3, 2):
            to = net.along(h, mod4(first_at[h] + d), then_at[h])
            first[h, d] = net.push(block, block, to, sends=first_sends)
    if late:
        yield
    for h in range(2):
        spread(h, 0)
    if not late:
        yield
    for j, d in ((1, 1), (2, 3), (3, 2)):
        for h in range(2):
            first[h, d].wait_recv()
            spread(h, j)
    yield
    if late:
        for j in range(4):
            for h in range(2):
                hand_over(h, j)
        yield
        for copy in over.values():
            copy.wait_recv()
        yield
        return
    for j in range(4):
        for h in range(2):
            hand_over(h, j)
        yield
        if j > 0:
            for h in range(2):
                over[h, j - 1].wait_recv()
            yield
    for h in range(2):
        over[h, 3].wait_recv()
    yield


def rows_of(parts, width):
    count = len(parts)
    rows = list(parts)
    if count < 8:
        rows.append(jnp.zeros((8 - count, width), F32))
    return jnp.concatenate(rows, axis=0)


def col_sum(t):
    return jnp.sum(t, axis=0, keepdims=True)


def split3(t):
    hi = t.astype(BF16)
    rest = t - hi.astype(F32)
    mid = rest.astype(BF16)
    lo = (rest - mid.astype(F32)).astype(BF16)
    zero = jnp.zeros((5, t.shape[1]), F32)
    return jnp.concatenate([hi.astype(F32), mid.astype(F32), lo.astype(F32), zero], axis=0).astype(BF16)


STAGES = ((1, 7), (2, 6), (3, 5), (0, 4))


def body(
    views_hbm,
    gain_hbm,
    bias_hbm,
    w_hbm,
    gw_hbm,
    small,
    views_gradient,
    views,
    gain,
    bias,
    grad_weight,
    w,
    act,
    act_t,
    xhat,
    slope,
    stats,
    zacc,
    zbuf,
    zsum,
    zcb,
    colstat,
    kpart,
    krecv,
    kmine,
    kin,
    kown,
    kgat,
    rsum,
    rcore,
    rmine,
    rin,
    moved,
    dz,
    dgive,
    dkeep,
    drecv,
    dpart,
    din,
    dmid,
    dmid_in,
    dpre,
    lsend,
    lrecv,
    fstat,
    send_sems,
    recv_sems,
    load_sem,
):
    net = Net(send_sems, recv_sems)
    z, y, x, core, chip = net.z, net.y, net.x, net.core, net.chip
    load_views = pltpu.make_async_copy(views_hbm, views, load_sem.at[0])
    load_gain = pltpu.make_async_copy(gain_hbm, gain, load_sem.at[1])
    load_bias = pltpu.make_async_copy(bias_hbm, bias, load_sem.at[2])
    load = pltpu.make_async_copy(w_hbm, w, load_sem.at[3])
    load_views.start()
    barrier = pltpu.get_barrier_semaphore()
    peers = net.peers()
    for peer in peers:
        pl.semaphore_signal(barrier, inc=1, device_id=peer, device_id_type=MESH)
    load_gain.start()
    load_bias.start()
    load.start()
    load_views.wait()
    local = []
    for v in range(2):
        t = views[v].astype(F32)
        m = col_sum(t) / 128.0
        local.append((m, col_sum((t - m) * (t - m))))
    stats[z] = rows_of([local[0][0], local[1][0], local[0][1], local[1][1]], 128)
    pl.semaphore_wait(barrier, len(peers))

    g = share_z(net, stats)
    next(g)
    load_gain.wait()
    load_bias.wait()
    next(g)
    inverse = []
    for v in range(2):
        m = stats[:, v, :]
        mean = col_sum(m) / PLANES
        spread = col_sum(stats[:, 2 + v, :] + 128.0 * (m - mean) * (m - mean))
        inv = 1.0 / jnp.sqrt(spread / ROWS + eps_norm)
        inverse.append(inv)
        xh = (views[v].astype(F32) - mean) * inv
        pre = gain[...] * xh + bias[...]
        inner = 0.7978845608028654 * (pre + 0.044715 * (pre * pre * pre))
        th = jnp.tanh(inner)
        a = 0.5 * pre * (1.0 + th)
        act[y, x, core, v] = a.astype(BF16).reshape(2, 4, 16, 128)
        xhat[v] = xh
        slope[v] = 0.5 * (1.0 + th) + 0.5 * pre * (1.0 - th * th) * (
            0.7978845608028654 * (1.0 + 3.0 * 0.044715 * (pre * pre))
        )

    def z_terms(j):
        for h in range(2):
            if h == 0:
                f = mod4(x + (0, 3, 1, 2)[j])
                lhs = [act[k, f, q, 0].reshape(128, 128) for k in range(4) for q in range(2)]
                rhs = w[:, f].reshape(1024, 256)
            else:
                f = mod4(y + (0, 3, 1, 2)[j])
                lhs = [act[f, k, q, 1].reshape(128, 128) for k in range(4) for q in range(2)]
                rhs = w[f].reshape(1024, 256)
            term = dot_nn(jnp.concatenate(lhs, axis=1), rhs)
            if j == 0:
                zacc[h] = term
            else:
                zacc[h] = zacc[h] + term

    ag = gather_plane(net, act)
    next(ag)
    next(ag)
    next(ag)
    load.wait()
    for j in range(3):
        next(ag)
        next(ag)
        z_terms(j)
    next(ag)

    row_v, row_s, row_q = lax.div(chip, 8), lax.rem(lax.div(chip, 4), 2), lax.rem(chip, 4)

    def feature_rows(plane):
        owner = plane * 2 + core
        return act.at[lax.div(owner, 4), lax.rem(owner, 4), :, row_v, row_s, row_q]

    z_terms(3)
    zb = zacc[...].astype(BF16)
    zbuf[z] = zb.reshape(4, 64, 256)
    zf = zb.astype(F32)
    zsums = [col_sum(zf[v])[:, k : k + 128] for v in range(2) for k in (0, 128)]
    zsum[z] = jnp.concatenate(zsums, axis=0)
    means = share_z(net, zsum)
    next(means)
    own_rows = act_t.at[y, x, core, :, lax.div(z, 4), lax.rem(z, 4)]
    zring = ring_z(net, zbuf)
    next(zring)
    features = net.group(kgat.at[0, 0, 0:14])
    for d in (4, 3, 5, 2, 6, 1, 7):
        net.push(feature_rows(mod8(z + d)), own_rows, net.at_z(d), features)
    own_rows[...] = feature_rows(z)[...]
    colstat[...] = jnp.zeros_like(colstat)

    def block_in(stage, owner, v):
        slot = mod8(z + STAGES[stage][owner])
        zc = zbuf[slot, 2 * v : 2 * v + 2].reshape(128, 256).astype(F32) - zmean[v]
        cb = zc.astype(BF16)
        zcb[slot, v] = cb
        cf = cb.astype(F32)
        colstat[v : v + 1, :] += col_sum(zc * zc)
        colstat[2 + v : 3 + v, :] += col_sum(cf * cf)
        colstat[4 + v : 5 + v, :] += col_sum(cf)
        kpart[stage, owner, 8 * v : 8 * v + 8] = dot_nt(zcb[z, v], cb).reshape(8, 16, 128)

    k_over, k_in, k_gat, k_done = {}, {}, {}, {}
    k_sends = [
        net.sends(m) for m in (kpart.at[:, 0], kin, kgat.at[:, 0, 0:15], kgat.at[0:3, 0])
    ]

    def k_give(stage):
        k_over[stage] = net.push(
            kpart.at[stage, 1 - core], krecv.at[stage], net.partner(), sends=k_sends[0]
        )

    def k_spread(stage):
        k_over[stage].wait_recv()
        kmine[stage] = kpart[stage, core] + krecv[stage]
        group = net.group(kin.at[stage], k_sends[1])
        for k, (dy, dx) in enumerate(OFFSETS):
            ty, tx = mod4(y + dy), mod4(x + dx)
            net.push(kmine.at[stage, ty * SIDE + tx], kin.at[stage, k], net.at(ty, tx), group)
        k_in[stage] = group[2]

    def k_gather(stage):
        k_in[stage].wait_recv()
        total = kmine[stage, chip] + jnp.sum(kin[stage], axis=0)
        kown[stage] = total
        kgat[stage, core, chip] = total.astype(BF16)
        own = kgat.at[stage, core, chip]
        group = net.group(kgat.at[stage, core, 0:15], k_sends[2])
        both = net.group(kgat.at[stage, core]) if stage == 3 else None
        for dy, dx in OFFSETS:
            ty, tx = mod4(y + dy), mod4(x + dx)
            net.push(own, own, net.at(ty, tx), group)
            if both is not None:
                net.push(own, own, net.other(ty, tx), both)
        if both is not None:
            net.push(own, own, net.partner(), both)
            k_done[stage] = both[2]
        k_gat[stage] = group[2]

    def k_hand(stage):
        k_gat[stage].wait_recv()
        k_done[stage] = net.push(
            kgat.at[stage, core], kgat.at[stage, core], net.partner(), sends=k_sends[3]
        )

    def k_moved(stage):
        k_done[stage].wait_recv()
        slots = [mod8(z + r) for r in STAGES[stage]]
        for v in range(2):
            lhs = jnp.concatenate(
                [kgat[stage, q, 8 * v : 8 * v + 8].reshape(128, 128) for q in range(2)], axis=1
            )
            rhs = jnp.concatenate([zcb[slots[0], v], zcb[slots[1], v]], axis=0)
            term = dot_nn(lhs, rhs)
            if stage == 0:
                moved[v] = term
            else:
                moved[v] = moved[v] + term

    def step(count):
        for _ in range(count):
            next(zring)

    def blocks(stage):
        for v in range(2):
            block_in(stage, 0, v)
            block_in(stage, 1, v)

    step(6)
    next(means)
    ztotal = [
        jnp.concatenate([col_sum(zsum[:, 2 * v + k, :]) for k in range(2)], axis=1) for v in range(2)
    ]
    zmean = [t / ROWS for t in ztotal]
    block_in(3, 0, 0)
    block_in(3, 0, 1)
    blocks(0)
    k_give(0)
    step(2)
    blocks(1)
    k_give(1)
    k_spread(0)
    step(1)
    features[2].wait_recv()
    agt = gather_plane(net, act_t, late=True)
    next(agt)
    step(2)
    k_spread(1)
    step(1)
    blocks(2)
    k_give(2)
    step(1)
    k_gather(0)
    k_spread(2)
    step(1)
    block_in(3, 1, 0)
    block_in(3, 1, 1)
    k_give(3)
    k_spread(3)

    for v in range(2):
        total = split3(colstat[4 + v : 5 + v, :])
        r = col_sum(dot_nt(total, zcb[:, v].reshape(1024, 256)))
        for slot in range(PLANES):
            rsum[v * PLANES + slot : v * PLANES + slot + 1, :] = r[:, 128 * slot : 128 * slot + 128]
    r_over = net.push(rsum, rcore, net.partner())
    k_gather(1)
    k_hand(0)
    k_gather(2)
    r_over.wait_recv()
    rmine[...] = rsum[...] + rcore[...]
    r_in = share_plane(net, rmine, rin)
    k_gather(3)
    next(agt)
    k_hand(1)
    k_moved(0)
    k_hand(2)
    k_moved(1)
    r_in.wait_recv()
    row_total = rmine[...] + jnp.sum(rin[...], axis=0)
    std, diag, mean_t = [], [], []
    for v in range(2):
        std.append(jnp.sqrt(colstat[v : v + 1, :] / (ROWS - 1) + eps_std))
        diag.append(colstat[2 + v : 3 + v, :])
        row = jnp.concatenate(
            [row_total[v * PLANES + slot : v * PLANES + slot + 1, :] for slot in range(PLANES)], axis=1
        )
        m = col_sum(dot_nn(split3(row), zcb[:, v].reshape(1024, 256)))
        hinge = jnp.where(std[v] < 1.0, hinge_coef, 0.0) / std[v]
        mean_t.append(
            (
                coef * (m - diag[v] * colstat[4 + v : 5 + v, :])
                - hinge * (ztotal[v] - ROWS * zmean[v])
            )
            / ROWS
        )
    k_moved(2)
    k_gat[3].wait_recv()
    k_moved(3)
    zl = [zbuf[z, 2 * v : 2 * v + 2].reshape(128, 256).astype(F32) for v in range(2)]
    diff = zl[0] - zl[1]
    for v in range(2):
        hinge = jnp.where(std[v] < 1.0, hinge_coef, 0.0) / std[v]
        t = coef * (moved[v] - zcb[z, v].astype(F32) * diag[v]) - hinge * (zl[v] - zmean[v])
        sign = 1.0 if v == 0 else -1.0
        d = (t - mean_t[v] + (sign * inv_coef) * diff).astype(BF16)
        dz[z, 2 * v : 2 * v + 2] = d.reshape(2, 4, 16, 256)

    dring = ring_z(net, dz)
    next(dring)
    first_at, then_at = (x, y), (y, x)
    dzl = [dz[z, 2 * v : 2 * v + 2].reshape(128, 256) for v in range(2)]
    d_over, d_in, d_mid = {}, {}, {}
    d_sends = [net.sends(dgive), net.sends(dpart.at[:, 1:4]), net.sends(dmid_in)]

    def d_terms(h, g, parity, store):
        f = mod4(first_at[h] + g)
        rows = w[:, f, parity] if h == 0 else w[f, :, parity]
        t = dot_nt(dzl[h], rows.reshape(512, 256))
        for k in range(4):
            store[h, g, k] = t[:, 128 * k : 128 * k + 128]

    def d_ready(h, g):
        d_over[h, g].wait_recv()
        if g > 0:
            dpart[h, g] = (dkeep[h, g] + drecv[h, g]).astype(BF16)

    def d_send(h, g, pieces):
        to = net.along(h, mod4(first_at[h] + g), then_at[h])
        for k in pieces:
            t = mod4(then_at[h] + k)
            net.push(dpart.at[h, g, t], din.at[h, g - 1, t], to, d_in[h, k])

    for h in range(2):
        for k in range(4):
            d_in[h, k] = net.group(din.at[h, :, 0], d_sends[1])
    last = None
    for g in (2, 1, 3, 0):
        for h in range(2):
            d_terms(h, g, 1 - core, dgive)
            d_over[h, g] = net.push(
                dgive.at[h, g], drecv.at[h, g], net.partner(), sends=d_sends[0]
            )
        for h in range(2):
            d_terms(h, g, core, dkeep)
        if last is not None:
            for h in range(2):
                d_ready(h, last)
                d_send(h, last, (2, 1))
        if g == 3:
            next(dring)
        last = g
    for g in (2, 1, 3):
        for h in range(2):
            d_send(h, g, (3, 0))
    next(dring)
    next(dring)
    for h in range(2):
        d_ready(h, 0)
    next(dring)

    def d_sum(h, k):
        t = mod4(then_at[h] + k)
        d_in[h, k][2].wait_recv()
        dmid[h, t] = (dkeep[h, 0, t] + drecv[h, 0, t]) + (
            din[h, 0, t].astype(F32) + din[h, 1, t].astype(F32) + din[h, 2, t].astype(F32)
        )
        if k > 0:
            net.push(
                dmid.at[h, t], dmid_in.at[h, k - 1], net.along(h, first_at[h], t), d_mid[h]
            )

    for h in range(2):
        d_mid[h] = net.group(dmid_in.at[h], d_sends[2])

    inv_row = col_sum(diff * diff)
    hinge_row = jnp.maximum(1.0 - std[0], 0.0) + jnp.maximum(1.0 - std[1], 0.0)
    diag_row = diag[0] * diag[0] + diag[1] * diag[1]
    wide = (25.0 / (ROWS * E)) * inv_row + (
        (25.0 / (2 * E)) * hinge_row - (1.0 / denom) * diag_row
    ) / PLANES
    ksq = col_sum(jnp.sum(kown[...] * kown[...], axis=0))
    share = wide[:, 0:128] + wide[:, 128:256] + (1.0 / denom) * ksq
    lsend[0] = rows_of([share], 128)
    loss_core = net.push(lsend.at[0], lrecv.at[15], net.partner())
    next(dring)
    for h in range(2):
        d_sum(h, 2)
    next(dring)
    for h in range(2):
        d_sum(h, 1)
    next(dring)
    loss_core.wait_recv()
    lsend[1] = lsend[0] + lrecv[15]
    loss_in = share_plane(net, lsend.at[1], lrecv.at[0:15])
    next(dring)
    for h in range(2):
        d_sum(h, 3)
    next(dring)
    for h in range(2):
        d_sum(h, 0)
    next(dring)
    next(dring)
    next(agt)
    loss_in.wait_recv()
    plane_loss = lsend[1, 0:1, :] + jnp.sum(lrecv[0:15, 0:1, :], axis=0)
    next(dring)
    sums = []
    for h in range(2):
        d_mid[h][2].wait_recv()
        d_act = dmid[h, then_at[h]] + dmid_in[h, 0] + dmid_in[h, 1] + dmid_in[h, 2]
        dp = d_act * slope[h]
        dpre[h] = dp
        sums.append((col_sum(dp), col_sum(dp * xhat[h])))
    fstat[z] = rows_of([sums[0][0], sums[1][0], sums[0][1], sums[1][1], plane_loss], 128)
    final = share_z(net, fstat)
    next(final)
    next(dring)
    next(dring)
    next(agt)

    def gw_step(i, carry):
        lhs, rhs = [], []
        for k in range(4):
            c = 4 * i + k
            cy, cx = lax.div(c, 4), lax.rem(c, 4)
            lhs.append(
                jnp.concatenate(
                    [act_t[cy, cx, q // 2, q % 2].reshape(128, 128) for q in range(4)], axis=1
                )
            )
            rhs.append(dz[:, cy, cx].reshape(128, 256))
        term = dot_tn(jnp.concatenate(lhs, axis=0), jnp.concatenate(rhs, axis=0))
        grad_weight[...] = jnp.where(i == 0, term, grad_weight[...] + term)
        return carry

    grad_weight[...] = jnp.zeros_like(grad_weight)
    lax.fori_loop(0, 4, gw_step, 0)
    put = pltpu.make_async_copy(grad_weight, gw_hbm, load_sem.at[4])
    put.start()
    next(final)
    total_b = [col_sum(fstat[:, v, :]) for v in range(2)]
    total_g = [col_sum(fstat[:, 2 + v, :]) for v in range(2)]
    small[...] = rows_of([total_g[0] + total_g[1], total_b[0] + total_b[1], col_sum(fstat[:, 4, :])], 128)
    for v in range(2):
        views_gradient[v] = (gain[...] * inverse[v]) * (
            dpre[v] - total_b[v] / ROWS - xhat[v] * (total_g[v] / ROWS)
        )
    put.wait()
    for copy in net.open:
        copy.wait_send()


SENDS = 24
RECEIVES = 142


def finish(gw_in, small, vg_in, loss, grad_weight, grad_gain, grad_bias, views_gradient):
    grad_weight[...] = gw_in[...]
    views_gradient[...] = vg_in[...]
    grad_gain[...] = small[0:1, :]
    grad_bias[...] = small[1:2, :]
    loss[0, 0] = jnp.sum(small[2:3, :])


def shards(views, norm_scale_gain, norm_shift_bias, weight):
    vmem = pltpu.VMEM
    scratch = [
        vmem((2, 128, 128), BF16),
        vmem((1, 128), F32),
        vmem((1, 128), F32),
        vmem((512, 256), F32),
        vmem((4, 4, 2, 128, 256), BF16),
        vmem((4, 4, 2, 2, 2, 4, 16, 128), BF16),
        vmem((4, 4, 2, 2, 2, 4, 16, 128), BF16),
        vmem((2, 128, 128), F32),
        vmem((2, 128, 128), F32),
        vmem((8, 8, 128), F32),
        vmem((2, 128, 256), F32),
        vmem((8, 4, 64, 256), BF16),
        vmem((8, 4, 128), F32),
        vmem((8, 2, 128, 256), BF16),
        vmem((8, 256), F32),
        vmem((4, 2, 16, 16, 128), F32),
        vmem((4, 16, 16, 128), F32),
        vmem((4, 16, 16, 128), F32),
        vmem((4, 15, 16, 128), F32),
        vmem((4, 16, 128), F32),
        vmem((4, 2, 16, 16, 128), BF16),
        vmem((16, 128), F32),
        vmem((16, 128), F32),
        vmem((16, 128), F32),
        vmem((15, 16, 128), F32),
        vmem((2, 128, 256), F32),
        vmem((8, 4, 4, 16, 256), BF16),
        vmem((2, 4, 4, 128, 128), F32),
        vmem((2, 4, 4, 128, 128), F32),
        vmem((2, 4, 4, 128, 128), F32),
        vmem((2, 4, 4, 128, 128), BF16),
        vmem((2, 3, 4, 128, 128), BF16),
        vmem((2, 4, 128, 128), F32),
        vmem((2, 3, 128, 128), F32),
        vmem((2, 128, 128), F32),
        vmem((2, 8, 128), F32),
        vmem((16, 8, 128), F32),
        vmem((8, 8, 128), F32),
        pltpu.SemaphoreType.DMA((SENDS,)),
        pltpu.SemaphoreType.DMA((RECEIVES,)),
        pltpu.SemaphoreType.DMA((5,)),
    ]
    whole = pl.BlockSpec(memory_space=pltpu.VMEM)
    made = (
        jax.ShapeDtypeStruct((512, 256), F32),
        jax.ShapeDtypeStruct((8, 128), F32),
        jax.ShapeDtypeStruct((2, 128, 128), F32),
    )
    results = pl.pallas_call(
        body,
        out_shape=made,
        in_specs=[pl.BlockSpec(memory_space=pl.ANY)] * 4,
        out_specs=(pl.BlockSpec(memory_space=pl.ANY), whole, whole),
        scratch_shapes=scratch,
        compiler_params=pltpu.CompilerParams(collective_id=0, has_side_effects=True),
        name="vicreg_step",
    )(
        views,
        norm_scale_gain.reshape(1, 128),
        norm_shift_bias.reshape(1, 128),
        weight.reshape(4, 4, 2, 128, 256),
    )
    loss, grad_weight, grad_gain, grad_bias, views_gradient = pl.pallas_call(
        finish,
        out_shape=(
            jax.ShapeDtypeStruct((1, 1), F32),
            made[0],
            jax.ShapeDtypeStruct((1, 128), F32),
            jax.ShapeDtypeStruct((1, 128), F32),
            made[2],
        ),
        in_specs=[whole, whole, whole],
        out_specs=(pl.BlockSpec(memory_space=pltpu.SMEM), whole, whole, whole, whole),
        name="write_results",
    )(*results)
    return (
        loss.reshape(()),
        grad_weight,
        grad_gain.reshape(128),
        grad_bias.reshape(128),
        views_gradient,
    )


def solution(mesh):
    placed = (P(None, "batch", "col"), P("col"), P("col"), P(None, "col"))
    return jax.shard_map(
        shards,
        mesh=mesh,
        in_specs=placed,
        out_specs=(P(), P("batch", "col"), P("col"), P("col"), P(None, "batch", "col")),
        check_vma=False,
    )
```
